32 devices in a mesh: shot: 4 (over y, core), depth: 8 (over z, x).
Axes of the slice: x: 2, y: 2, z: 4, core: 2. Of those that a mesh axis runs over, the one named last changes fastest.
Arguments:
- grad_part: float32 [4, 256, 8192], P('shot', 'depth'), may hold values from -6 to 6
- illum_part: float32 [4, 256, 8192], P('shot', 'depth'), may hold values from 0.1 to 1
- source_count: int32 [4], P('shot'), may hold values from 1 to 8
- rate: float32 [8192], P('shot'), may hold values from 0.00078125 to 0.03
- coef_table: float32 [64], replicated, may hold values from 0.2 to 1
- coef_index: int32 [256], P('depth'), may hold values from 0 to 63
Outputs:
- image: float32 [256, 8192], P('depth', 'shot')
The draws below stay inside these ranges and needn't reach their ends.
All inputs are finite; a program needn't handle non-finite values.
Results may differ from the reference program's by a relative error of at most 0.0003.
Values sent between devices are 32-bit elements; how exact they have to be, the bound alone decides.
A program may use at most 64 MiB of HBM per device.

```python
import math
import jax
import jax.numpy as jnp
from jax import lax

LAT = 8192
SRC = 8
NTAB = 64
NZ = 256
GROUPS = 4


def with_ends(array, own_key, low, top_value):
    index_at = [jax.random.randint(jax.random.fold_in(own_key, axis), (), 0, length) for axis, length in enumerate(array.shape)]
    main_axis = array.shape.index(max(array.shape))
    neighbour = index_at[:main_axis] + [(index_at[main_axis] + 1) % array.shape[main_axis]] + index_at[main_axis + 1:]
    return array.at[tuple(index_at)].set(low).at[tuple(neighbour)].set(top_value)


def spiked(result, key, source, target, shards_of, factor):
    owner, partner = [(jnp.arange(result.shape[axis_at]) // (result.shape[axis_at] // shards_of)).reshape([-1 if axis == axis_at else 1 for axis in range(result.ndim)]) for axis_at in (source, target)]
    chosen = jax.random.permutation(key, shards_of)[partner]
    strong = (owner == chosen) | (owner == (partner + shards_of // 2) % shards_of)
    return jnp.where(strong, factor * result, result)


def level_of(rng, shape, shards, low, largest):
    level, own = 1.0, jax.random.fold_in(rng, 6)
    for position, shards_of in shards:
        draws = jnp.exp(jax.random.uniform(jax.random.fold_in(own, position), (shards_of,), jnp.float32, low / len(shards), largest / len(shards)))
        level = level * jnp.repeat(draws, shape[position] // shards_of).reshape([-1 if axis == position else 1 for axis in range(len(shape))])
    return level


def noise_with(stream_key, shape, scale, limit, pieces, heavy, held_as=jnp.bfloat16):
    drawn = scale * jax.random.normal(stream_key, shape, jnp.float32)
    if pieces:
        drawn = drawn * level_of(stream_key, shape, pieces, -0.22, 0.18)
    return jnp.clip(spiked(drawn, jax.random.fold_in(stream_key, 3), *heavy), -limit, limit).astype(held_as)


def setup_inputs(seed: int = 0) -> dict:
    arg_keys = jax.random.split(jax.random.key(seed), 7)
    grad_part = noise_with(arg_keys[0], (GROUPS, NZ, LAT), 1.0, 6.0, ((0, 4), (1, 8)), (0, 2, 4, 2.0), jnp.float32)
    illum_part = jnp.clip(jnp.exp(math.log(1.0) - 2.3025851 * jax.random.uniform(arg_keys[1], (GROUPS, NZ, LAT), jnp.float32) ** level_of(arg_keys[1], (GROUPS, NZ, LAT), ((0, 4), (1, 8)), -0.2, 0.2)), 0.1, 1.0)
    source_count = with_ends(jax.random.randint(arg_keys[2], (GROUPS,), 1, SRC + 1), jax.random.fold_in(arg_keys[2], 1), 1, SRC).astype(jnp.int32)
    rate = jnp.clip(jnp.exp(math.log(0.03) - 3.6480574 * jax.random.uniform(arg_keys[3], (LAT,), jnp.float32) ** level_of(arg_keys[3], (LAT,), ((0, 4),), -0.2, 0.2)), 0.00078125, 0.03)
    coef_table = jnp.clip(jnp.exp(jax.random.uniform(arg_keys[4], (NTAB,), jnp.float32, math.log(0.2), math.log(1.0))), 0.2, 1.0)
    coef_index = with_ends(jax.random.randint(arg_keys[5], (NZ,), 0, NTAB), jax.random.fold_in(arg_keys[5], 1), 0, NTAB - 1).astype(jnp.int32)
    return {"grad_part": grad_part, "illum_part": illum_part, "source_count": source_count, "rate": rate, "coef_table": coef_table, "coef_index": coef_index}


def combine(earlier, later):
    return (earlier[0] * later[0], later[0] * earlier[1] + later[1])


def reference(grad_part, illum_part, source_count, rate, coef_table, coef_index):
    weight = 1.0 / source_count.astype(jnp.float32)
    scaled = grad_part * weight[:, None, None]
    summed = jnp.sum(scaled, axis=0)
    lights = jnp.sum(illum_part, axis=0)
    quotient = summed / lights
    picked = coef_table[coef_index]
    factor = jnp.exp(-(picked[:, None] * rate[None, :]))
    _, smooth = lax.associative_scan(combine, (factor, (1.0 - factor) * quotient), axis=0)
    _, image = lax.associative_scan(combine, (factor, (1.0 - factor) * smooth), reverse=True, axis=0)
    return image
```

```python
import functools

import jax
import jax.numpy as jnp
from jax import lax
from jax.experimental import pallas as pl
from jax.experimental.pallas import tpu as pltpu
from jax.sharding import PartitionSpec as P

MESH = pl.DeviceIdType.MESH
LANES = 128
SUB = 8
RELAYS = ()


def body(
    dims,
    grad, illum, count, rate_hbm, table_hbm, index_hbm, out,
    both, sums, landed, early, inject, weigh, back, reach, held, states,
    rate, table, index, mine_count, mate_count, *rest,
):
    ys, ks, rows, width, chunks, sending, taking = dims
    relays = [ch for ch in sending if chunks[ch][2]]
    late, rest = rest[: len(chunks)], rest[len(chunks) :]
    via, rest = dict(zip(relays, rest)), rest[len(relays) :]
    (
        got, part_send, sums_send, sums_recv, via_recv, via_send,
        early_send, early_recv, late_send, late_recv, w_send, w_recv, small_sem, word,
    ) = rest
    tiles = rows // SUB
    me = lax.axis_index("shot")
    d = lax.axis_index("depth")
    y, c = me // 2, me % 2
    mate = y * 2 + 1 - c

    def peer(j):
        return j + (d <= j).astype(jnp.int32)

    def other(i):
        return lax.rem(y + i, ys)

    def greet(semaphore):
        flip = d + 1 - 2 * lax.rem(d, 2)
        pl.semaphore_signal(semaphore, inc=1, device_id=(me, flip), device_id_type=MESH)
        for step in (2, -2):
            near = d + step

            @pl.when((near >= 0) & (near < ks))
            def _():
                pl.semaphore_signal(semaphore, inc=1, device_id=(me, near), device_id_type=MESH)

    def greeted(semaphore, more):
        inner = (d >= 2).astype(jnp.int32) + (d < ks - 2).astype(jnp.int32)
        pl.semaphore_wait(semaphore, inner + 1 + more)

    def relayed(ch, at):
        low, high = chunks[ch][2]
        return (at >= low) & (at < high)

    barrier = pltpu.get_barrier_semaphore()
    pl.semaphore_signal(barrier, inc=1, device_id=(mate, d), device_id_type=MESH)
    for i in range(1, ys):
        pl.semaphore_signal(barrier, inc=1, device_id=(other(i) * 2 + c, d), device_id_type=MESH)
    greet(barrier)
    expected = ys
    if relays:
        expected = expected + (d >= 2).astype(jnp.int32) * (ys - 1)

        @pl.when(d < ks - 2)
        def _():
            for i in range(1, ys):
                pl.semaphore_signal(barrier, inc=1, device_id=(other(i) * 2 + c, d + 2), device_id_type=MESH)

    def columns(ch):
        return pl.ds(chunks[ch][0] * LANES, chunks[ch][1] * LANES)

    def fetch(i, start, cols, semaphore):
        into = pl.ds(i * width + start * LANES, cols * LANES)
        for a, src in enumerate((grad, illum)):
            at = pl.multiple_of((other(i) * 2 + c) * width + start * LANES, LANES)
            pltpu.make_async_copy(
                src.at[0, :, pl.ds(at, cols * LANES)], both.at[0, a, :, into], semaphore
            ).start()

    def give(i, start, cols, semaphore):
        into = pl.ds(i * width + start * LANES, cols * LANES)
        for a, src in enumerate((grad, illum)):
            at = pl.multiple_of((other(i) * 2 + 1 - c) * width + start * LANES, LANES)
            pltpu.make_async_remote_copy(
                src_ref=src.at[0, :, pl.ds(at, cols * LANES)],
                dst_ref=both.at[1, a, :, into],
                send_sem=part_send,
                recv_sem=semaphore,
                device_id=(mate, d),
                device_id_type=MESH,
            ).start()

    def wait_for(ref, semaphore):
        pltpu.make_async_copy(ref, ref, semaphore).wait()

    def arrived(i, start, cols, semaphore):
        wait_for(both.at[:, :, :, pl.ds(i * width + start * LANES, cols * LANES)], semaphore)

    def sums_copy(i, ch):
        return pltpu.make_async_remote_copy(
            src_ref=sums.at[i - 1, :, :, columns(ch)],
            dst_ref=landed.at[i - 1, :, :, columns(ch)],
            send_sem=sums_send,
            recv_sem=sums_recv.at[ch],
            device_id=(other(i) * 2 + c, d),
            device_id_type=MESH,
        )

    def relay_copy(i, ch):
        return pltpu.make_async_remote_copy(
            src_ref=sums.at[i - 1, :, :, columns(ch)],
            dst_ref=via[ch].at[i - 1],
            send_sem=sums_send,
            recv_sem=via_recv.at[relays.index(ch)],
            device_id=(other(i) * 2 + c, d - 2),
            device_id_type=MESH,
        )

    def forward(ch):
        @pl.when(relayed(ch, d + 2))
        def _():
            wait_for(via[ch], via_recv.at[relays.index(ch)])
            for i in range(1, ys):
                pltpu.make_async_remote_copy(
                    src_ref=via[ch].at[i - 1],
                    dst_ref=landed.at[i - 1, :, :, columns(ch)],
                    send_sem=via_send.at[relays.index(ch)],
                    recv_sem=sums_recv.at[ch],
                    device_id=(me, d + 2),
                    device_id_type=MESH,
                ).start()

    def carry_copy(buffer, send, recv, j):
        return pltpu.make_async_remote_copy(
            src_ref=buffer.at[d],
            dst_ref=buffer.at[d],
            send_sem=send,
            recv_sem=recv,
            device_id=(me, peer(j)),
            device_id_type=MESH,
        )

    w_copy = pltpu.make_async_remote_copy(
        src_ref=count,
        dst_ref=mate_count,
        send_sem=w_send,
        recv_sem=w_recv,
        device_id=(mate, d),
        device_id_type=MESH,
    )

    def small_copies():
        pairs = ((count, mine_count), (table_hbm, table), (index_hbm, index), (rate_hbm, rate))
        return [pltpu.make_async_copy(a, b, small_sem.at[n]) for n, (a, b) in enumerate(pairs)]

    first_part = [(i, ch) for ch in sending for i in range(1, ys)]
    for n, (i, ch) in enumerate(first_part):
        fetch(i, *chunks[ch][:2], got.at[n])
    for copy in small_copies():
        copy.start()

    greeted(barrier, expected)
    w_copy.start()
    for n, (i, ch) in enumerate(first_part):
        give(i, *chunks[ch][:2], got.at[n])

    rounds = ks // 2 - 1
    greet(word.at[0])

    def pass_on(r):
        greeted(word.at[r], 0)
        if r + 1 < rounds:
            greet(word.at[r + 1])

    sub = lax.broadcasted_iota(jnp.int32, (SUB, LANES), 0)

    def prefix(v):
        for s in (1, 2, 4):
            v = v + jnp.where(sub >= s, pltpu.roll(v, s, 0), 0.0)
        return v

    def suffix(v):
        for s in (1, 2, 4):
            v = v + jnp.where(sub < SUB - s, pltpu.roll(v, SUB - s, 0), 0.0)
        return v

    def first(v):
        return jnp.broadcast_to(v[0:1], (SUB, LANES))

    def last(v):
        return jnp.broadcast_to(v[SUB - 1 : SUB], (SUB, LANES))

    entries = table.shape[1]

    def upright(row):
        n = row.shape[1]
        diagonal = lax.broadcasted_iota(jnp.int32, (n, n), 0) == lax.broadcasted_iota(
            jnp.int32, (n, n), 1
        )
        return jnp.sum(
            jnp.where(diagonal, jnp.broadcast_to(row, (n, n)), 0.0), axis=1, keepdims=True
        )

    def depths():
        level = lax.broadcasted_iota(jnp.int32, (entries, rows), 0)
        hit = jnp.broadcast_to(index[...], (entries, rows)) == level
        spread = jnp.broadcast_to(upright(table[...]), (entries, rows))
        picked = upright(jnp.sum(jnp.where(hit, spread, 0.0), axis=0, keepdims=True))
        coef, through, before = [], [], []
        total = jnp.zeros((SUB, LANES), jnp.float32)
        for t in range(tiles):
            v = jnp.broadcast_to(picked[t * SUB : (t + 1) * SUB], (SUB, LANES))
            run = prefix(v) + total
            coef.append(v)
            through.append(run)
            before.append(run - v)
            total = last(run)
        return coef, through, before, total

    def terms():
        coef, through, before, total = depths()
        for j in range(width // LANES):
            at = pl.ds(j * LANES, LANES)
            r = jnp.broadcast_to(rate[0:1, at], (SUB, LANES))
            tail = jnp.zeros((SUB, LANES), jnp.float32)
            for t in reversed(range(tiles)):
                zs = pl.ds(t * SUB, SUB)
                rest = 1.0 - jnp.exp(-(coef[t] * r))
                inject[zs, at] = rest * jnp.exp(through[t] * r)
                h = rest * jnp.exp(-((through[t] + before[t]) * r))
                weigh[zs, at] = h
                lift = jnp.exp(before[t] * r)
                back[zs, at] = lift
                run = suffix(h) + tail
                reach[zs, at] = lift * run
                tail = first(run)
            early[d, 0, pl.ds(j, 1), :] = jnp.exp(-(total * r))[0:1]
            early[d, 1, pl.ds(j, 1), :] = tail[0:1]

    copies = small_copies()
    copies[0].wait()
    w_copy.wait_recv()

    def weight(ref):
        return 1.0 / jnp.full((SUB, LANES), ref[0]).astype(jnp.float32)

    w, v = weight(mine_count), weight(mate_count)

    def reduced(i, a, zs, at):
        at = pl.ds(i * width + at.start, at.size)
        if a == 0:
            return both[0, 0, zs, at] * w + both[1, 0, zs, at] * v
        return both[0, 1, zs, at] + both[1, 1, zs, at]

    def lanes(ch):
        return [pl.ds((chunks[ch][0] + j) * LANES, LANES) for j in range(chunks[ch][1])]

    for n, (i, ch) in enumerate(first_part):
        arrived(i, *chunks[ch][:2], got.at[n])
        for at in lanes(ch):
            for t in range(tiles):
                zs = pl.ds(t * SUB, SUB)
                for a in range(2):
                    sums[i - 1, a, zs, at] = reduced(i, a, zs, at)
        if ch in relays:
            pl.when(relayed(ch, d))(relay_copy(i, ch).start)
            pl.when(jnp.logical_not(relayed(ch, d)))(sums_copy(i, ch).start)
        else:
            sums_copy(i, ch).start()
        if n == 0:
            pass_on(0)

    local = len(first_part)
    fetch(0, 0, width // LANES, got.at[local])
    give(0, 0, width // LANES, got.at[local])
    if rounds > 1:
        pass_on(1)
    for copy in copies[1:]:
        copy.wait()
    terms()
    for r in range(2, rounds):
        pass_on(r)
    for j in range(ks - 1):
        carry_copy(early, early_send, early_recv, j).start()

    arrived(0, 0, width // LANES, got.at[local])
    for n, ch in enumerate(taking):
        start, cols, _ = chunks[ch]
        wait_for(landed.at[:, :, :, columns(ch)], sums_recv.at[ch])
        for j, at in enumerate(lanes(ch)):
            carry = jnp.zeros((SUB, LANES), jnp.float32)
            parts = []
            for t in range(tiles):
                zs = pl.ds(t * SUB, SUB)
                num, den = reduced(0, 0, zs, at), reduced(0, 1, zs, at)
                for i in range(1, ys):
                    num = num + landed[i - 1, 0, zs, at]
                    den = den + landed[i - 1, 1, zs, at]
                run = prefix(inject[zs, at] * (num / den)) + carry
                parts.append(run)
                carry = last(run)
            row = pl.ds(start + j, 1)
            late[ch][d, pl.ds(j, 1), :] = carry[0:1] * early[d, 0, row, :]
            tail = jnp.zeros((SUB, LANES), jnp.float32)
            for t in reversed(range(tiles)):
                zs = pl.ds(t * SUB, SUB)
                run = suffix(weigh[zs, at] * parts[t]) + tail
                held[zs, at] = run
                tail = first(run)
            late[ch][d, pl.ds(cols + j, 1), :] = tail[0:1]
        for j in range(ks - 1):
            carry_copy(late[ch], late_send.at[ch], late_recv.at[ch], j).start()
        if n == 0:
            for r in relays:
                forward(r)

    others = pl.ds(0, ks - 1)
    wait_for(early.at[others], early_recv)
    for ch in taking:
        wait_for(late[ch].at[others], late_recv.at[ch])
        start, cols, _ = chunks[ch]
        rs = pl.ds(start, cols)
        down, lift = pl.ds(0, cols), pl.ds(cols, cols)
        state = jnp.zeros((cols, LANES), jnp.float32)
        mine = state
        ups = []
        for k in range(ks):
            mine = jnp.where(k == d, state, mine)
            ups.append(late[ch][k, lift] + early[k, 1, rs] * state)
            if k < ks - 1:
                state = late[ch][k, down] + early[k, 0, rs] * state
        up = jnp.zeros((cols, LANES), jnp.float32)
        for k in reversed(range(1, ks)):
            up = jnp.where(k > d, ups[k] + early[k, 0, rs] * up, up)
        states[0, rs] = mine
        states[1, rs] = up * early[d, 0, rs]
        for j, at in enumerate(lanes(ch)):
            row = pl.ds(start + j, 1)
            e = jnp.broadcast_to(states[0, row, :], (SUB, LANES))
            b = jnp.broadcast_to(states[1, row, :], (SUB, LANES))
            for t in range(tiles):
                zs = pl.ds(t * SUB, SUB)
                out[zs, at] = back[zs, at] * (held[zs, at] + b) + reach[zs, at] * e

    w_copy.wait_send()
    wait_for(both.at[1], part_send)
    wait_for(sums, sums_send)
    for ch in relays:
        pl.when(relayed(ch, d + 2))(
            functools.partial(wait_for, via[ch], via_send.at[relays.index(ch)])
        )
    wait_for(early.at[others], early_send)
    for ch in taking:
        wait_for(late[ch].at[others], late_send.at[ch])


def split(blocks, ys, ks):
    edge = max(1, blocks // 8)
    hops = RELAYS if ys == 2 and ks >= 6 and blocks >= 16 else ()
    inner = blocks - 2 * edge - sum(n for n, _ in hops)
    sizes = [edge, *(n for n, _ in hops), inner - inner // 2, inner // 2, edge]
    ways = [None, *(way(ks) for _, way in hops), None, None, None]
    found = [(sum(sizes[:n]), size, ways[n]) for n, size in enumerate(sizes) if size]
    sending = list(range(len(found)))
    direct = [n for n in sending if not found[n][2]]
    taking = [*direct[:-1], *(n for n in sending if found[n][2]), direct[-1]]
    return found, sending, taking


def shards(ys, ks, grad_part, illum_part, source_count, rate, coef_table, coef_index):
    _, rows, lateral = grad_part.shape
    width = lateral // (2 * ys)
    blocks = width // LANES
    chunks, sending, taking = split(blocks, ys, ks)
    relays = [chunk for chunk in chunks if chunk[2]]
    f32, i32 = jnp.float32, jnp.int32
    dma = pltpu.SemaphoreType.DMA
    sent = pltpu.VMEM((ys - 1, 2, rows, width), f32)
    field = pltpu.VMEM((rows, width), f32)
    anywhere = pl.BlockSpec(memory_space=pl.ANY)
    small = (rate.reshape(1, -1), coef_table.reshape(1, -1), coef_index.reshape(1, -1))
    return pl.pallas_call(
        functools.partial(body, (ys, ks, rows, width, chunks, sending, taking)),
        out_shape=jax.ShapeDtypeStruct((rows, width), f32),
        in_specs=[anywhere] * 6,
        out_specs=pl.BlockSpec(memory_space=pltpu.VMEM),
        scratch_shapes=[
            pltpu.VMEM((2, 2, rows, ys * width), f32),
            sent,
            sent,
            pltpu.VMEM((ks, 2, blocks, LANES), f32),
            field, field, field, field, field,
            pltpu.VMEM((2, blocks, LANES), f32),
            pltpu.VMEM(small[0].shape, f32),
            pltpu.VMEM(small[1].shape, f32),
            pltpu.VMEM(small[2].shape, i32),
            pltpu.SMEM((1,), i32),
            pltpu.SMEM((1,), i32),
            *[pltpu.VMEM((ks, 2 * n, LANES), f32) for _, n, _ in chunks],
            *[pltpu.VMEM((ys - 1, 2, rows, n * LANES), f32) for _, n, _ in relays],
            dma(((ys - 1) * len(chunks) + 1,)),
            dma,
            dma,
            dma((len(chunks),)),
            dma((max(1, len(relays)),)),
            dma((max(1, len(relays)),)),
            dma,
            dma,
            dma((len(chunks),)),
            dma((len(chunks),)),
            dma,
            dma,
            dma((4,)),
            pltpu.SemaphoreType.REGULAR((ks // 2 - 1,)),
        ],
        compiler_params=pltpu.CompilerParams(collective_id=0, has_side_effects=True, vmem_limit_bytes=53 * 2**20),
    )(
        grad_part,
        illum_part,
        source_count,
        *[pltpu.with_memory_space_constraint(x, pltpu.HBM) for x in small],
    )


def solution(mesh):
    placed = (
        P("shot", "depth", None),
        P("shot", "depth", None),
        P("shot"),
        P("shot"),
        P(),
        P("depth"),
    )
    return jax.shard_map(
        functools.partial(shards, mesh.shape["shot"] // 2, mesh.shape["depth"]),
        mesh=mesh, in_specs=placed, out_specs=P("depth", "shot"), check_vma=False,
    )
```

```python
import functools

import jax
import jax.numpy as jnp
from jax import lax
from jax.experimental import pallas as pl
from jax.experimental.pallas import tpu as pltpu
from jax.sharding import PartitionSpec as P

MESH = pl.DeviceIdType.MESH
LANES = 128
SUB = 8
RELAYS = ((2, lambda ks: (2, ks)), (1, lambda ks: (ks - 4, ks - 2)))


def body(
    dims,
    grad, illum, count, rate_hbm, table_hbm, index_hbm, out,
    both, sums, landed, early, inject, weigh, back, reach, held, states,
    rate, table, index, mine_count, mate_count, *rest,
):
    ys, ks, rows, width, chunks, sending, taking = dims
    relays = [ch for ch in sending if chunks[ch][2]]
    late, rest = rest[: len(chunks)], rest[len(chunks) :]
    via, rest = dict(zip(relays, rest)), rest[len(relays) :]
    (
        got, part_send, sums_send, sums_recv, via_recv, via_send,
        early_send, early_recv, late_send, late_recv, w_send, w_recv, small_sem, word,
    ) = rest
    tiles = rows // SUB
    me = lax.axis_index("shot")
    d = lax.axis_index("depth")
    y, c = me // 2, me % 2
    mate = y * 2 + 1 - c

    def peer(j):
        return j + (d <= j).astype(jnp.int32)

    def other(i):
        return lax.rem(y + i, ys)

    def greet(semaphore):
        flip = d + 1 - 2 * lax.rem(d, 2)
        pl.semaphore_signal(semaphore, inc=1, device_id=(me, flip), device_id_type=MESH)
        for step in (2, -2):
            near = d + step

            @pl.when((near >= 0) & (near < ks))
            def _():
                pl.semaphore_signal(semaphore, inc=1, device_id=(me, near), device_id_type=MESH)

    def greeted(semaphore, more):
        inner = (d >= 2).astype(jnp.int32) + (d < ks - 2).astype(jnp.int32)
        pl.semaphore_wait(semaphore, inner + 1 + more)

    def relayed(ch, at):
        low, high = chunks[ch][2]
        return (at >= low) & (at < high)

    barrier = pltpu.get_barrier_semaphore()
    pl.semaphore_signal(barrier, inc=1, device_id=(mate, d), device_id_type=MESH)
    for i in range(1, ys):
        pl.semaphore_signal(barrier, inc=1, device_id=(other(i) * 2 + c, d), device_id_type=MESH)
    greet(barrier)
    expected = ys
    if relays:
        expected = expected + (d >= 2).astype(jnp.int32) * (ys - 1)

        @pl.when(d < ks - 2)
        def _():
            for i in range(1, ys):
                pl.semaphore_signal(barrier, inc=1, device_id=(other(i) * 2 + c, d + 2), device_id_type=MESH)

    def columns(ch):
        return pl.ds(chunks[ch][0] * LANES, chunks[ch][1] * LANES)

    def fetch(i, start, cols, semaphore):
        into = pl.ds(i * width + start * LANES, cols * LANES)
        for a, src in enumerate((grad, illum)):
            at = pl.multiple_of((other(i) * 2 + c) * width + start * LANES, LANES)
            pltpu.make_async_copy(
                src.at[0, :, pl.ds(at, cols * LANES)], both.at[0, a, :, into], semaphore
            ).start()

    def give(i, start, cols, semaphore):
        into = pl.ds(i * width + start * LANES, cols * LANES)
        for a, src in enumerate((grad, illum)):
            at = pl.multiple_of((other(i) * 2 + 1 - c) * width + start * LANES, LANES)
            pltpu.make_async_remote_copy(
                src_ref=src.at[0, :, pl.ds(at, cols * LANES)],
                dst_ref=both.at[1, a, :, into],
                send_sem=part_send,
                recv_sem=semaphore,
                device_id=(mate, d),
                device_id_type=MESH,
            ).start()

    def wait_for(ref, semaphore):
        pltpu.make_async_copy(ref, ref, semaphore).wait()

    def arrived(i, start, cols, semaphore):
        wait_for(both.at[:, :, :, pl.ds(i * width + start * LANES, cols * LANES)], semaphore)

    def sums_copy(i, ch):
        return pltpu.make_async_remote_copy(
            src_ref=sums.at[i - 1, :, :, columns(ch)],
            dst_ref=landed.at[i - 1, :, :, columns(ch)],
            send_sem=sums_send,
            recv_sem=sums_recv.at[ch],
            device_id=(other(i) * 2 + c, d),
            device_id_type=MESH,
        )

    def relay_copy(i, ch):
        return pltpu.make_async_remote_copy(
            src_ref=sums.at[i - 1, :, :, columns(ch)],
            dst_ref=via[ch].at[i - 1],
            send_sem=sums_send,
            recv_sem=via_recv.at[relays.index(ch)],
            device_id=(other(i) * 2 + c, d - 2),
            device_id_type=MESH,
        )

    def forward(ch):
        @pl.when(relayed(ch, d + 2))
        def _():
            wait_for(via[ch], via_recv.at[relays.index(ch)])
            for i in range(1, ys):
                pltpu.make_async_remote_copy(
                    src_ref=via[ch].at[i - 1],
                    dst_ref=landed.at[i - 1, :, :, columns(ch)],
                    send_sem=via_send.at[relays.index(ch)],
                    recv_sem=sums_recv.at[ch],
                    device_id=(me, d + 2),
                    device_id_type=MESH,
                ).start()

    def carry_copy(buffer, send, recv, j):
        return pltpu.make_async_remote_copy(
            src_ref=buffer.at[d],
            dst_ref=buffer.at[d],
            send_sem=send,
            recv_sem=recv,
            device_id=(me, peer(j)),
            device_id_type=MESH,
        )

    w_copy = pltpu.make_async_remote_copy(
        src_ref=count,
        dst_ref=mate_count,
        send_sem=w_send,
        recv_sem=w_recv,
        device_id=(mate, d),
        device_id_type=MESH,
    )

    def small_copies():
        pairs = ((count, mine_count), (table_hbm, table), (index_hbm, index), (rate_hbm, rate))
        return [pltpu.make_async_copy(a, b, small_sem.at[n]) for n, (a, b) in enumerate(pairs)]

    first_part = [(i, ch) for ch in sending for i in range(1, ys)]
    for n, (i, ch) in enumerate(first_part):
        fetch(i, *chunks[ch][:2], got.at[n])
    for copy in small_copies():
        copy.start()

    greeted(barrier, expected)
    w_copy.start()
    for n, (i, ch) in enumerate(first_part):
        give(i, *chunks[ch][:2], got.at[n])

    rounds = ks // 2 - 1
    greet(word.at[0])

    def pass_on(r):
        greeted(word.at[r], 0)
        if r + 1 < rounds:
            greet(word.at[r + 1])

    sub = lax.broadcasted_iota(jnp.int32, (SUB, LANES), 0)

    def prefix(v):
        for s in (1, 2, 4):
            v = v + jnp.where(sub >= s, pltpu.roll(v, s, 0), 0.0)
        return v

    def suffix(v):
        for s in (1, 2, 4):
            v = v + jnp.where(sub < SUB - s, pltpu.roll(v, SUB - s, 0), 0.0)
        return v

    def first(v):
        return jnp.broadcast_to(v[0:1], (SUB, LANES))

    def last(v):
        return jnp.broadcast_to(v[SUB - 1 : SUB], (SUB, LANES))

    entries = table.shape[1]

    def upright(row):
        n = row.shape[1]
        diagonal = lax.broadcasted_iota(jnp.int32, (n, n), 0) == lax.broadcasted_iota(
            jnp.int32, (n, n), 1
        )
        return jnp.sum(
            jnp.where(diagonal, jnp.broadcast_to(row, (n, n)), 0.0), axis=1, keepdims=True
        )

    def depths():
        level = lax.broadcasted_iota(jnp.int32, (entries, rows), 0)
        hit = jnp.broadcast_to(index[...], (entries, rows)) == level
        spread = jnp.broadcast_to(upright(table[...]), (entries, rows))
        picked = upright(jnp.sum(jnp.where(hit, spread, 0.0), axis=0, keepdims=True))
        coef, through, before = [], [], []
        total = jnp.zeros((SUB, LANES), jnp.float32)
        for t in range(tiles):
            v = jnp.broadcast_to(picked[t * SUB : (t + 1) * SUB], (SUB, LANES))
            run = prefix(v) + total
            coef.append(v)
            through.append(run)
            before.append(run - v)
            total = last(run)
        return coef, through, before, total

    def terms():
        coef, through, before, total = depths()
        for j in range(width // LANES):
            at = pl.ds(j * LANES, LANES)
            r = jnp.broadcast_to(rate[0:1, at], (SUB, LANES))
            tail = jnp.zeros((SUB, LANES), jnp.float32)
            for t in reversed(range(tiles)):
                zs = pl.ds(t * SUB, SUB)
                rest = 1.0 - jnp.exp(-(coef[t] * r))
                inject[zs, at] = rest * jnp.exp(through[t] * r)
                h = rest * jnp.exp(-((through[t] + before[t]) * r))
                weigh[zs, at] = h
                lift = jnp.exp(before[t] * r)
                back[zs, at] = lift
                run = suffix(h) + tail
                reach[zs, at] = lift * run
                tail = first(run)
            early[d, 0, pl.ds(j, 1), :] = jnp.exp(-(total * r))[0:1]
            early[d, 1, pl.ds(j, 1), :] = tail[0:1]

    copies = small_copies()
    copies[0].wait()
    w_copy.wait_recv()

    def weight(ref):
        return 1.0 / jnp.full((SUB, LANES), ref[0]).astype(jnp.float32)

    w, v = weight(mine_count), weight(mate_count)

    def reduced(i, a, zs, at):
        at = pl.ds(i * width + at.start, at.size)
        if a == 0:
            return both[0, 0, zs, at] * w + both[1, 0, zs, at] * v
        return both[0, 1, zs, at] + both[1, 1, zs, at]

    def lanes(ch):
        return [pl.ds((chunks[ch][0] + j) * LANES, LANES) for j in range(chunks[ch][1])]

    for n, (i, ch) in enumerate(first_part):
        arrived(i, *chunks[ch][:2], got.at[n])
        for at in lanes(ch):
            for t in range(tiles):
                zs = pl.ds(t * SUB, SUB)
                for a in range(2):
                    sums[i - 1, a, zs, at] = reduced(i, a, zs, at)
        if ch in relays:
            pl.when(relayed(ch, d))(relay_copy(i, ch).start)
            pl.when(jnp.logical_not(relayed(ch, d)))(sums_copy(i, ch).start)
        else:
            sums_copy(i, ch).start()
        if n == 0:
            pass_on(0)

    local = len(first_part)
    fetch(0, 0, width // LANES, got.at[local])
    give(0, 0, width // LANES, got.at[local])
    if rounds > 1:
        pass_on(1)
    for copy in copies[1:]:
        copy.wait()
    terms()
    for r in range(2, rounds):
        pass_on(r)
    for j in range(ks - 1):
        carry_copy(early, early_send, early_recv, j).start()

    arrived(0, 0, width // LANES, got.at[local])
    for n, ch in enumerate(taking):
        start, cols, _ = chunks[ch]
        wait_for(landed.at[:, :, :, columns(ch)], sums_recv.at[ch])
        for j, at in enumerate(lanes(ch)):
            carry = jnp.zeros((SUB, LANES), jnp.float32)
            parts = []
            for t in range(tiles):
                zs = pl.ds(t * SUB, SUB)
                num, den = reduced(0, 0, zs, at), reduced(0, 1, zs, at)
                for i in range(1, ys):
                    num = num + landed[i - 1, 0, zs, at]
                    den = den + landed[i - 1, 1, zs, at]
                run = prefix(inject[zs, at] * (num / den)) + carry
                parts.append(run)
                carry = last(run)
            row = pl.ds(start + j, 1)
            late[ch][d, pl.ds(j, 1), :] = carry[0:1] * early[d, 0, row, :]
            tail = jnp.zeros((SUB, LANES), jnp.float32)
            for t in reversed(range(tiles)):
                zs = pl.ds(t * SUB, SUB)
                run = suffix(weigh[zs, at] * parts[t]) + tail
                held[zs, at] = run
                tail = first(run)
            late[ch][d, pl.ds(cols + j, 1), :] = tail[0:1]
        for j in range(ks - 1):
            carry_copy(late[ch], late_send.at[ch], late_recv.at[ch], j).start()
        if n == 0:
            for r in relays:
                forward(r)

    others = pl.ds(0, ks - 1)
    wait_for(early.at[others], early_recv)
    for ch in taking:
        wait_for(late[ch].at[others], late_recv.at[ch])
        start, cols, _ = chunks[ch]
        rs = pl.ds(start, cols)
        down, lift = pl.ds(0, cols), pl.ds(cols, cols)
        state = jnp.zeros((cols, LANES), jnp.float32)
        mine = state
        ups = []
        for k in range(ks):
            mine = jnp.where(k == d, state, mine)
            ups.append(late[ch][k, lift] + early[k, 1, rs] * state)
            if k < ks - 1:
                state = late[ch][k, down] + early[k, 0, rs] * state
        up = jnp.zeros((cols, LANES), jnp.float32)
        for k in reversed(range(1, ks)):
            up = jnp.where(k > d, ups[k] + early[k, 0, rs] * up, up)
        states[0, rs] = mine
        states[1, rs] = up * early[d, 0, rs]
        for j, at in enumerate(lanes(ch)):
            row = pl.ds(start + j, 1)
            e = jnp.broadcast_to(states[0, row, :], (SUB, LANES))
            b = jnp.broadcast_to(states[1, row, :], (SUB, LANES))
            for t in range(tiles):
                zs = pl.ds(t * SUB, SUB)
                out[zs, at] = back[zs, at] * (held[zs, at] + b) + reach[zs, at] * e

    w_copy.wait_send()
    wait_for(both.at[1], part_send)
    wait_for(sums, sums_send)
    for ch in relays:
        pl.when(relayed(ch, d + 2))(
            functools.partial(wait_for, via[ch], via_send.at[relays.index(ch)])
        )
    wait_for(early.at[others], early_send)
    for ch in taking:
        wait_for(late[ch].at[others], late_send.at[ch])


def split(blocks, ys, ks):
    edge = max(1, blocks // 8)
    hops = RELAYS if ys == 2 and ks >= 6 and blocks >= 16 else ()
    inner = blocks - 2 * edge - sum(n for n, _ in hops)
    sizes = [edge, *(n for n, _ in hops), inner - inner // 2, inner // 2, edge]
    ways = [None, *(way(ks) for _, way in hops), None, None, None]
    found = [(sum(sizes[:n]), size, ways[n]) for n, size in enumerate(sizes) if size]
    sending = list(range(len(found)))
    direct = [n for n in sending if not found[n][2]]
    taking = [*direct[:-1], *(n for n in sending if found[n][2]), direct[-1]]
    return found, sending, taking


def shards(ys, ks, grad_part, illum_part, source_count, rate, coef_table, coef_index):
    _, rows, lateral = grad_part.shape
    width = lateral // (2 * ys)
    blocks = width // LANES
    chunks, sending, taking = split(blocks, ys, ks)
    relays = [chunk for chunk in chunks if chunk[2]]
    f32, i32 = jnp.float32, jnp.int32
    dma = pltpu.SemaphoreType.DMA
    sent = pltpu.VMEM((ys - 1, 2, rows, width), f32)
    field = pltpu.VMEM((rows, width), f32)
    anywhere = pl.BlockSpec(memory_space=pl.ANY)
    small = (rate.reshape(1, -1), coef_table.reshape(1, -1), coef_index.reshape(1, -1))
    return pl.pallas_call(
        functools.partial(body, (ys, ks, rows, width, chunks, sending, taking)),
        out_shape=jax.ShapeDtypeStruct((rows, width), f32),
        in_specs=[anywhere] * 6,
        out_specs=pl.BlockSpec(memory_space=pltpu.VMEM),
        scratch_shapes=[
            pltpu.VMEM((2, 2, rows, ys * width), f32),
            sent,
            sent,
            pltpu.VMEM((ks, 2, blocks, LANES), f32),
            field, field, field, field, field,
            pltpu.VMEM((2, blocks, LANES), f32),
            pltpu.VMEM(small[0].shape, f32),
            pltpu.VMEM(small[1].shape, f32),
            pltpu.VMEM(small[2].shape, i32),
            pltpu.SMEM((1,), i32),
            pltpu.SMEM((1,), i32),
            *[pltpu.VMEM((ks, 2 * n, LANES), f32) for _, n, _ in chunks],
            *[pltpu.VMEM((ys - 1, 2, rows, n * LANES), f32) for _, n, _ in relays],
            dma(((ys - 1) * len(chunks) + 1,)),
            dma,
            dma,
            dma((len(chunks),)),
            dma((max(1, len(relays)),)),
            dma((max(1, len(relays)),)),
            dma,
            dma,
            dma((len(chunks),)),
            dma((len(chunks),)),
            dma,
            dma,
            dma((4,)),
            pltpu.SemaphoreType.REGULAR((ks // 2 - 1,)),
        ],
        compiler_params=pltpu.CompilerParams(collective_id=0, has_side_effects=True, vmem_limit_bytes=53 * 2**20),
    )(
        grad_part,
        illum_part,
        source_count,
        *[pltpu.with_memory_space_constraint(x, pltpu.HBM) for x in small],
    )


def solution(mesh):
    placed = (
        P("shot", "depth", None),
        P("shot", "depth", None),
        P("shot"),
        P("shot"),
        P(),
        P("depth"),
    )
    return jax.shard_map(
        functools.partial(shards, mesh.shape["shot"] // 2, mesh.shape["depth"]),
        mesh=mesh, in_specs=placed, out_specs=P("depth", "shot"), check_vma=False,
    )
```

```python
import functools

import jax
import jax.numpy as jnp
from jax import lax
from jax.experimental import pallas as pl
from jax.experimental.pallas import tpu as pltpu
from jax.sharding import PartitionSpec as P

MESH = pl.DeviceIdType.MESH
LANES = 128
SUB = 8


def deep(at, ks):
    return (at >= 2) & (at < ks)


def middle(at, ks):
    return (at >= ks - 4) & (at < ks - 2)


def odd(at, ks):
    return lax.rem(at, 2) == 1


ROUTES = ((2, deep), (1, odd))
RELAYS = ((2, (2, deep)), (1, (2, middle)), (1, (1, odd)))


def body(
    dims,
    grad, illum, count, rate_hbm, table_hbm, index_hbm, out,
    both, sums, landed, early, inject, weigh, back, reach, held, states,
    rate, table, index, mine_count, mate_count, *rest,
):
    ys, ks, rows, width, chunks, sending, taking = dims
    relays = [ch for ch in sending if chunks[ch][2]]
    late, rest = rest[: len(chunks)], rest[len(chunks) :]
    via, rest = dict(zip(relays, rest)), rest[len(relays) :]
    (
        got, part_send, sums_send, sums_recv, via_recv, via_send,
        early_send, early_recv, late_send, late_recv, w_send, w_recv, small_sem, word,
    ) = rest
    tiles = rows // SUB
    me = lax.axis_index("shot")
    d = lax.axis_index("depth")
    y, c = me // 2, me % 2
    mate = y * 2 + 1 - c

    def peer(j):
        return j + (d <= j).astype(jnp.int32)

    def other(i):
        return lax.rem(y + i, ys)

    def greet(semaphore):
        flip = d + 1 - 2 * lax.rem(d, 2)
        pl.semaphore_signal(semaphore, inc=1, device_id=(me, flip), device_id_type=MESH)
        for step in (2, -2):
            near = d + step

            @pl.when((near >= 0) & (near < ks))
            def _():
                pl.semaphore_signal(semaphore, inc=1, device_id=(me, near), device_id_type=MESH)

    def neighbours():
        return (d >= 2).astype(jnp.int32) + (d < ks - 2).astype(jnp.int32) + 1

    def relayed(ch, at):
        return chunks[ch][2][1](at, ks)

    def stride(ch):
        return chunks[ch][2][0]

    barrier = pltpu.get_barrier_semaphore()
    pl.semaphore_signal(barrier, inc=1, device_id=(mate, d), device_id_type=MESH)
    for i in range(1, ys):
        pl.semaphore_signal(barrier, inc=1, device_id=(other(i) * 2 + c, d), device_id_type=MESH)
    pl.when(y == 0)(functools.partial(greet, barrier))
    expected = ys + (y == 0).astype(jnp.int32) * neighbours()
    for step, some in ROUTES if relays else ():
        expected = expected + some(d, ks).astype(jnp.int32) * (ys - 1)

        @pl.when(some(d + step, ks))
        def _():
            for i in range(1, ys):
                pl.semaphore_signal(barrier, inc=1, device_id=(other(i) * 2 + c, d + step), device_id_type=MESH)

    def columns(ch):
        return pl.ds(chunks[ch][0] * LANES, chunks[ch][1] * LANES)

    def fetch(i, start, cols, semaphore):
        into = pl.ds(i * width + start * LANES, cols * LANES)
        for a, src in enumerate((grad, illum)):
            at = pl.multiple_of((other(i) * 2 + c) * width + start * LANES, LANES)
            pltpu.make_async_copy(
                src.at[0, :, pl.ds(at, cols * LANES)], both.at[0, a, :, into], semaphore
            ).start()

    def give(i, start, cols, semaphore):
        into = pl.ds(i * width + start * LANES, cols * LANES)
        for a, src in enumerate((grad, illum)):
            at = pl.multiple_of((other(i) * 2 + 1 - c) * width + start * LANES, LANES)
            pltpu.make_async_remote_copy(
                src_ref=src.at[0, :, pl.ds(at, cols * LANES)],
                dst_ref=both.at[1, a, :, into],
                send_sem=part_send,
                recv_sem=semaphore,
                device_id=(mate, d),
                device_id_type=MESH,
            ).start()

    def wait_for(ref, semaphore):
        pltpu.make_async_copy(ref, ref, semaphore).wait()

    def arrived(i, start, cols, semaphore):
        wait_for(both.at[:, :, :, pl.ds(i * width + start * LANES, cols * LANES)], semaphore)

    def sums_copy(i, ch):
        return pltpu.make_async_remote_copy(
            src_ref=sums.at[i - 1, :, :, columns(ch)],
            dst_ref=landed.at[i - 1, :, :, columns(ch)],
            send_sem=sums_send,
            recv_sem=sums_recv.at[ch],
            device_id=(other(i) * 2 + c, d),
            device_id_type=MESH,
        )

    def relay_copy(i, ch):
        return pltpu.make_async_remote_copy(
            src_ref=sums.at[i - 1, :, :, columns(ch)],
            dst_ref=via[ch].at[i - 1],
            send_sem=sums_send,
            recv_sem=via_recv.at[relays.index(ch)],
            device_id=(other(i) * 2 + c, d - stride(ch)),
            device_id_type=MESH,
        )

    def forward(ch):
        @pl.when(relayed(ch, d + stride(ch)))
        def _():
            wait_for(via[ch], via_recv.at[relays.index(ch)])
            for i in range(1, ys):
                pltpu.make_async_remote_copy(
                    src_ref=via[ch].at[i - 1],
                    dst_ref=landed.at[i - 1, :, :, columns(ch)],
                    send_sem=via_send.at[relays.index(ch)],
                    recv_sem=sums_recv.at[ch],
                    device_id=(me, d + stride(ch)),
                    device_id_type=MESH,
                ).start()

    def carry_copy(buffer, send, recv, j):
        return pltpu.make_async_remote_copy(
            src_ref=buffer.at[d],
            dst_ref=buffer.at[d],
            send_sem=send,
            recv_sem=recv,
            device_id=(me, peer(j)),
            device_id_type=MESH,
        )

    w_copy = pltpu.make_async_remote_copy(
        src_ref=count,
        dst_ref=mate_count,
        send_sem=w_send,
        recv_sem=w_recv,
        device_id=(mate, d),
        device_id_type=MESH,
    )

    def small_copies():
        pairs = ((count, mine_count), (table_hbm, table), (index_hbm, index), (rate_hbm, rate))
        return [pltpu.make_async_copy(a, b, small_sem.at[n]) for n, (a, b) in enumerate(pairs)]

    first_part = [(i, ch) for ch in sending for i in range(1, ys)]
    for n, (i, ch) in enumerate(first_part):
        fetch(i, *chunks[ch][:2], got.at[n])
    for copy in small_copies():
        copy.start()

    pl.semaphore_wait(barrier, expected)
    w_copy.start()
    for n, (i, ch) in enumerate(first_part):
        give(i, *chunks[ch][:2], got.at[n])

    rounds = ks // 2
    pl.when(y == 0)(functools.partial(greet, word.at[0]))

    def pass_on(r):
        @pl.when(y == 0)
        def _():
            pl.semaphore_wait(word.at[r], neighbours())
            if r + 1 < rounds:
                greet(word.at[r + 1])
            else:
                for i in range(1, ys):
                    pl.semaphore_signal(
                        word.at[rounds], inc=1, device_id=(other(i) * 2 + c, d), device_id_type=MESH
                    )

        if r + 1 == rounds:
            pl.when(y != 0)(lambda: pl.semaphore_wait(word.at[rounds], 1))

    sub = lax.broadcasted_iota(jnp.int32, (SUB, LANES), 0)

    def prefix(v):
        for s in (1, 2, 4):
            v = v + jnp.where(sub >= s, pltpu.roll(v, s, 0), 0.0)
        return v

    def suffix(v):
        for s in (1, 2, 4):
            v = v + jnp.where(sub < SUB - s, pltpu.roll(v, SUB - s, 0), 0.0)
        return v

    def first(v):
        return jnp.broadcast_to(v[0:1], (SUB, LANES))

    def last(v):
        return jnp.broadcast_to(v[SUB - 1 : SUB], (SUB, LANES))

    entries = table.shape[1]

    def upright(row):
        n = row.shape[1]
        diagonal = lax.broadcasted_iota(jnp.int32, (n, n), 0) == lax.broadcasted_iota(
            jnp.int32, (n, n), 1
        )
        return jnp.sum(
            jnp.where(diagonal, jnp.broadcast_to(row, (n, n)), 0.0), axis=1, keepdims=True
        )

    def depths():
        level = lax.broadcasted_iota(jnp.int32, (entries, rows), 0)
        hit = jnp.broadcast_to(index[...], (entries, rows)) == level
        spread = jnp.broadcast_to(upright(table[...]), (entries, rows))
        picked = upright(jnp.sum(jnp.where(hit, spread, 0.0), axis=0, keepdims=True))
        coef, through, before = [], [], []
        total = jnp.zeros((SUB, LANES), jnp.float32)
        for t in range(tiles):
            v = jnp.broadcast_to(picked[t * SUB : (t + 1) * SUB], (SUB, LANES))
            run = prefix(v) + total
            coef.append(v)
            through.append(run)
            before.append(run - v)
            total = last(run)
        return coef, through, before, total

    def terms():
        coef, through, before, total = depths()
        for j in range(width // LANES):
            at = pl.ds(j * LANES, LANES)
            r = jnp.broadcast_to(rate[0:1, at], (SUB, LANES))
            tail = jnp.zeros((SUB, LANES), jnp.float32)
            for t in reversed(range(tiles)):
                zs = pl.ds(t * SUB, SUB)
                rest = 1.0 - jnp.exp(-(coef[t] * r))
                inject[zs, at] = rest * jnp.exp(through[t] * r)
                h = rest * jnp.exp(-((through[t] + before[t]) * r))
                weigh[zs, at] = h
                lift = jnp.exp(before[t] * r)
                back[zs, at] = lift
                run = suffix(h) + tail
                reach[zs, at] = lift * run
                tail = first(run)
            early[d, 0, pl.ds(j, 1), :] = jnp.exp(-(total * r))[0:1]
            early[d, 1, pl.ds(j, 1), :] = tail[0:1]

    copies = small_copies()
    copies[0].wait()
    w_copy.wait_recv()

    def weight(ref):
        return 1.0 / jnp.full((SUB, LANES), ref[0]).astype(jnp.float32)

    w, v = weight(mine_count), weight(mate_count)

    def reduced(i, a, zs, at):
        at = pl.ds(i * width + at.start, at.size)
        if a == 0:
            return both[0, 0, zs, at] * w + both[1, 0, zs, at] * v
        return both[0, 1, zs, at] + both[1, 1, zs, at]

    def lanes(ch):
        return [pl.ds((chunks[ch][0] + j) * LANES, LANES) for j in range(chunks[ch][1])]

    for n, (i, ch) in enumerate(first_part):
        arrived(i, *chunks[ch][:2], got.at[n])
        for at in lanes(ch):
            for t in range(tiles):
                zs = pl.ds(t * SUB, SUB)
                for a in range(2):
                    sums[i - 1, a, zs, at] = reduced(i, a, zs, at)
        if ch in relays:
            pl.when(relayed(ch, d))(relay_copy(i, ch).start)
            pl.when(jnp.logical_not(relayed(ch, d)))(sums_copy(i, ch).start)
        else:
            sums_copy(i, ch).start()
        if n == 0:
            pass_on(0)

    local = len(first_part)
    fetch(0, 0, width // LANES, got.at[local])
    give(0, 0, width // LANES, got.at[local])
    if rounds > 1:
        pass_on(1)
    for copy in copies[1:]:
        copy.wait()
    terms()
    for r in range(2, rounds):
        pass_on(r)
    for j in range(ks - 1):
        carry_copy(early, early_send, early_recv, j).start()

    arrived(0, 0, width // LANES, got.at[local])
    for n, ch in enumerate(taking):
        start, cols, _ = chunks[ch]
        wait_for(landed.at[:, :, :, columns(ch)], sums_recv.at[ch])
        for j, at in enumerate(lanes(ch)):
            carry = jnp.zeros((SUB, LANES), jnp.float32)
            parts = []
            for t in range(tiles):
                zs = pl.ds(t * SUB, SUB)
                num, den = reduced(0, 0, zs, at), reduced(0, 1, zs, at)
                for i in range(1, ys):
                    num = num + landed[i - 1, 0, zs, at]
                    den = den + landed[i - 1, 1, zs, at]
                run = prefix(inject[zs, at] * (num / den)) + carry
                parts.append(run)
                carry = last(run)
            row = pl.ds(start + j, 1)
            late[ch][d, pl.ds(j, 1), :] = carry[0:1] * early[d, 0, row, :]
            tail = jnp.zeros((SUB, LANES), jnp.float32)
            for t in reversed(range(tiles)):
                zs = pl.ds(t * SUB, SUB)
                run = suffix(weigh[zs, at] * parts[t]) + tail
                held[zs, at] = run
                tail = first(run)
            late[ch][d, pl.ds(cols + j, 1), :] = tail[0:1]
        for j in range(ks - 1):
            carry_copy(late[ch], late_send.at[ch], late_recv.at[ch], j).start()
        if n == 0:
            for r in relays:
                forward(r)

    others = pl.ds(0, ks - 1)
    wait_for(early.at[others], early_recv)
    for ch in taking:
        wait_for(late[ch].at[others], late_recv.at[ch])
        start, cols, _ = chunks[ch]
        rs = pl.ds(start, cols)
        down, lift = pl.ds(0, cols), pl.ds(cols, cols)
        state = jnp.zeros((cols, LANES), jnp.float32)
        mine = state
        ups = []
        for k in range(ks):
            mine = jnp.where(k == d, state, mine)
            ups.append(late[ch][k, lift] + early[k, 1, rs] * state)
            if k < ks - 1:
                state = late[ch][k, down] + early[k, 0, rs] * state
        up = jnp.zeros((cols, LANES), jnp.float32)
        for k in reversed(range(1, ks)):
            up = jnp.where(k > d, ups[k] + early[k, 0, rs] * up, up)
        states[0, rs] = mine
        states[1, rs] = up * early[d, 0, rs]
        for j, at in enumerate(lanes(ch)):
            row = pl.ds(start + j, 1)
            e = jnp.broadcast_to(states[0, row, :], (SUB, LANES))
            b = jnp.broadcast_to(states[1, row, :], (SUB, LANES))
            for t in range(tiles):
                zs = pl.ds(t * SUB, SUB)
                out[zs, at] = back[zs, at] * (held[zs, at] + b) + reach[zs, at] * e

    w_copy.wait_send()
    wait_for(both.at[1], part_send)
    wait_for(sums, sums_send)
    for ch in relays:
        pl.when(relayed(ch, d + stride(ch)))(
            functools.partial(wait_for, via[ch], via_send.at[relays.index(ch)])
        )
    wait_for(early.at[others], early_send)
    for ch in taking:
        wait_for(late[ch].at[others], late_send.at[ch])


def split(blocks, ys, ks):
    edge = max(1, blocks // 8)
    hops = RELAYS if ys == 2 and ks >= 6 and blocks >= 16 else ()
    inner = blocks - 2 * edge - sum(n for n, _ in hops)
    sizes = [edge, *(n for n, _ in hops), inner - inner // 2, inner // 2, edge]
    ways = [None, *(way for _, way in hops), None, None, None]
    found = [(sum(sizes[:n]), size, ways[n]) for n, size in enumerate(sizes) if size]
    sending = list(range(len(found)))
    direct = [n for n in sending if not found[n][2]]
    taking = [*direct[:-1], *(n for n in sending if found[n][2]), direct[-1]]
    return found, sending, taking


def shards(ys, ks, grad_part, illum_part, source_count, rate, coef_table, coef_index):
    _, rows, lateral = grad_part.shape
    width = lateral // (2 * ys)
    blocks = width // LANES
    chunks, sending, taking = split(blocks, ys, ks)
    relays = [chunk for chunk in chunks if chunk[2]]
    f32, i32 = jnp.float32, jnp.int32
    dma = pltpu.SemaphoreType.DMA
    sent = pltpu.VMEM((ys - 1, 2, rows, width), f32)
    field = pltpu.VMEM((rows, width), f32)
    anywhere = pl.BlockSpec(memory_space=pl.ANY)
    small = (rate.reshape(1, -1), coef_table.reshape(1, -1), coef_index.reshape(1, -1))
    return pl.pallas_call(
        functools.partial(body, (ys, ks, rows, width, chunks, sending, taking)),
        out_shape=jax.ShapeDtypeStruct((rows, width), f32),
        in_specs=[anywhere] * 6,
        out_specs=pl.BlockSpec(memory_space=pltpu.VMEM),
        scratch_shapes=[
            pltpu.VMEM((2, 2, rows, ys * width), f32),
            sent,
            sent,
            pltpu.VMEM((ks, 2, blocks, LANES), f32),
            field, field, field, field, field,
            pltpu.VMEM((2, blocks, LANES), f32),
            pltpu.VMEM(small[0].shape, f32),
            pltpu.VMEM(small[1].shape, f32),
            pltpu.VMEM(small[2].shape, i32),
            pltpu.SMEM((1,), i32),
            pltpu.SMEM((1,), i32),
            *[pltpu.VMEM((ks, 2 * n, LANES), f32) for _, n, _ in chunks],
            *[pltpu.VMEM((ys - 1, 2, rows, n * LANES), f32) for _, n, _ in relays],
            dma(((ys - 1) * len(chunks) + 1,)),
            dma,
            dma,
            dma((len(chunks),)),
            dma((max(1, len(relays)),)),
            dma((max(1, len(relays)),)),
            dma,
            dma,
            dma((len(chunks),)),
            dma((len(chunks),)),
            dma,
            dma,
            dma((4,)),
            pltpu.SemaphoreType.REGULAR((ks // 2 + 1,)),
        ],
        compiler_params=pltpu.CompilerParams(collective_id=0, has_side_effects=True, vmem_limit_bytes=53 * 2**20),
    )(
        grad_part,
        illum_part,
        source_count,
        *[pltpu.with_memory_space_constraint(x, pltpu.HBM) for x in small],
    )


def solution(mesh):
    placed = (
        P("shot", "depth", None),
        P("shot", "depth", None),
        P("shot"),
        P("shot"),
        P(),
        P("depth"),
    )
    return jax.shard_map(
        functools.partial(shards, mesh.shape["shot"] // 2, mesh.shape["depth"]),
        mesh=mesh, in_specs=placed, out_specs=P("depth", "shot"), check_vma=False,
    )
```

```python
import functools

import jax
import jax.numpy as jnp
from jax import lax
from jax.experimental import pallas as pl
from jax.experimental.pallas import tpu as pltpu
from jax.sharding import PartitionSpec as P

MESH = pl.DeviceIdType.MESH
LANES = 128
SUB = 8


def deep(at, ks):
    return (at >= 2) & (at < ks)


def middle(at, ks):
    return (at >= ks - 4) & (at < ks - 2)


def odd(at, ks):
    return lax.rem(at, 2) == 1


ROUTES = ((2, deep), (1, odd))
RELAYS = ((2, (2, deep)), (1, (2, middle)), (1, (1, odd)))


def body(
    dims,
    grad, illum, count, rate_hbm, table_hbm, index_hbm, out,
    both, sums, landed, early, inject, weigh, back, reach, held, states,
    rate, table, index, mine_count, mate_count, *rest,
):
    ys, ks, rows, width, chunks, sending, taking = dims
    relays = [ch for ch in sending if chunks[ch][2]]
    late, rest = rest[: len(chunks)], rest[len(chunks) :]
    via, rest = dict(zip(relays, rest)), rest[len(relays) :]
    (
        got, part_send, sums_send, sums_recv, via_recv, via_send,
        early_send, early_recv, late_send, late_recv, w_send, w_recv, small_sem, word,
    ) = rest
    tiles = rows // SUB
    me = lax.axis_index("shot")
    d = lax.axis_index("depth")
    y, c = me // 2, me % 2
    mate = y * 2 + 1 - c

    def peer(j):
        return j + (d <= j).astype(jnp.int32)

    def other(i):
        return lax.rem(y + i, ys)

    def greet(semaphore):
        flip = d + 1 - 2 * lax.rem(d, 2)
        pl.semaphore_signal(semaphore, inc=1, device_id=(me, flip), device_id_type=MESH)
        for step in (2, -2):
            near = d + step

            @pl.when((near >= 0) & (near < ks))
            def _():
                pl.semaphore_signal(semaphore, inc=1, device_id=(me, near), device_id_type=MESH)

    def neighbours():
        return (d >= 2).astype(jnp.int32) + (d < ks - 2).astype(jnp.int32) + 1

    def relayed(ch, at):
        return chunks[ch][2][1](at, ks)

    def stride(ch):
        return chunks[ch][2][0]

    barrier = pltpu.get_barrier_semaphore()
    pl.semaphore_signal(barrier, inc=1, device_id=(mate, d), device_id_type=MESH)
    for i in range(1, ys):
        pl.semaphore_signal(barrier, inc=1, device_id=(other(i) * 2 + c, d), device_id_type=MESH)
    pl.when(y == 0)(functools.partial(greet, barrier))
    expected = ys + (y == 0).astype(jnp.int32) * neighbours()
    for step, some in ROUTES if relays else ():
        expected = expected + some(d, ks).astype(jnp.int32) * (ys - 1)

        @pl.when(some(d + step, ks))
        def _():
            for i in range(1, ys):
                pl.semaphore_signal(barrier, inc=1, device_id=(other(i) * 2 + c, d + step), device_id_type=MESH)

    def columns(ch):
        return pl.ds(chunks[ch][0] * LANES, chunks[ch][1] * LANES)

    def fetch(i, start, cols, semaphore):
        into = pl.ds(i * width + start * LANES, cols * LANES)
        for a, src in enumerate((grad, illum)):
            at = pl.multiple_of((other(i) * 2 + c) * width + start * LANES, LANES)
            pltpu.make_async_copy(
                src.at[0, :, pl.ds(at, cols * LANES)], both.at[0, a, :, into], semaphore
            ).start()

    def give(i, start, cols, semaphore):
        into = pl.ds(i * width + start * LANES, cols * LANES)
        for a, src in enumerate((grad, illum)):
            at = pl.multiple_of((other(i) * 2 + 1 - c) * width + start * LANES, LANES)
            pltpu.make_async_remote_copy(
                src_ref=src.at[0, :, pl.ds(at, cols * LANES)],
                dst_ref=both.at[1, a, :, into],
                send_sem=part_send,
                recv_sem=semaphore,
                device_id=(mate, d),
                device_id_type=MESH,
            ).start()

    def wait_for(ref, semaphore):
        pltpu.make_async_copy(ref, ref, semaphore).wait()

    def arrived(i, start, cols, semaphore):
        wait_for(both.at[:, :, :, pl.ds(i * width + start * LANES, cols * LANES)], semaphore)

    def sums_copy(i, ch):
        return pltpu.make_async_remote_copy(
            src_ref=sums.at[i - 1, :, :, columns(ch)],
            dst_ref=landed.at[i - 1, :, :, columns(ch)],
            send_sem=sums_send,
            recv_sem=sums_recv.at[ch],
            device_id=(other(i) * 2 + c, d),
            device_id_type=MESH,
        )

    def relay_copy(i, ch):
        return pltpu.make_async_remote_copy(
            src_ref=sums.at[i - 1, :, :, columns(ch)],
            dst_ref=via[ch].at[i - 1],
            send_sem=sums_send,
            recv_sem=via_recv.at[relays.index(ch)],
            device_id=(other(i) * 2 + c, d - stride(ch)),
            device_id_type=MESH,
        )

    def forward(ch):
        @pl.when(relayed(ch, d + stride(ch)))
        def _():
            wait_for(via[ch], via_recv.at[relays.index(ch)])
            for i in range(1, ys):
                pltpu.make_async_remote_copy(
                    src_ref=via[ch].at[i - 1],
                    dst_ref=landed.at[i - 1, :, :, columns(ch)],
                    send_sem=via_send.at[relays.index(ch)],
                    recv_sem=sums_recv.at[ch],
                    device_id=(me, d + stride(ch)),
                    device_id_type=MESH,
                ).start()

    def carry_copy(buffer, send, recv, j):
        return pltpu.make_async_remote_copy(
            src_ref=buffer.at[d],
            dst_ref=buffer.at[d],
            send_sem=send,
            recv_sem=recv,
            device_id=(me, peer(j)),
            device_id_type=MESH,
        )

    w_copy = pltpu.make_async_remote_copy(
        src_ref=count,
        dst_ref=mate_count,
        send_sem=w_send,
        recv_sem=w_recv,
        device_id=(mate, d),
        device_id_type=MESH,
    )

    def small_copies():
        pairs = ((count, mine_count), (table_hbm, table), (index_hbm, index), (rate_hbm, rate))
        return [pltpu.make_async_copy(a, b, small_sem.at[n]) for n, (a, b) in enumerate(pairs)]

    first_part = [(i, ch) for ch in sending for i in range(1, ys)]
    for n, (i, ch) in enumerate(first_part):
        fetch(i, *chunks[ch][:2], got.at[n])
    for copy in small_copies():
        copy.start()

    pl.semaphore_wait(barrier, expected)
    w_copy.start()
    for n, (i, ch) in enumerate(first_part):
        give(i, *chunks[ch][:2], got.at[n])

    rounds = ks // 2
    pl.when(y == 0)(functools.partial(greet, word.at[0]))

    def pass_on(r):
        @pl.when(y == 0)
        def _():
            pl.semaphore_wait(word.at[r], neighbours())
            if r + 1 < rounds:
                greet(word.at[r + 1])
            else:
                for i in range(1, ys):
                    pl.semaphore_signal(
                        word.at[rounds], inc=1, device_id=(other(i) * 2 + c, d), device_id_type=MESH
                    )

        if r + 1 == rounds:
            pl.when(y != 0)(lambda: pl.semaphore_wait(word.at[rounds], 1))

    sub = lax.broadcasted_iota(jnp.int32, (SUB, LANES), 0)

    def prefix(v):
        for s in (1, 2, 4):
            v = v + jnp.where(sub >= s, pltpu.roll(v, s, 0), 0.0)
        return v

    def suffix(v):
        for s in (1, 2, 4):
            v = v + jnp.where(sub < SUB - s, pltpu.roll(v, SUB - s, 0), 0.0)
        return v

    def first(v):
        return jnp.broadcast_to(v[0:1], (SUB, LANES))

    def last(v):
        return jnp.broadcast_to(v[SUB - 1 : SUB], (SUB, LANES))

    entries = table.shape[1]

    def upright(row):
        n = row.shape[1]
        diagonal = lax.broadcasted_iota(jnp.int32, (n, n), 0) == lax.broadcasted_iota(
            jnp.int32, (n, n), 1
        )
        return jnp.sum(
            jnp.where(diagonal, jnp.broadcast_to(row, (n, n)), 0.0), axis=1, keepdims=True
        )

    def depths():
        level = lax.broadcasted_iota(jnp.int32, (entries, rows), 0)
        hit = jnp.broadcast_to(index[...], (entries, rows)) == level
        spread = jnp.broadcast_to(upright(table[...]), (entries, rows))
        picked = upright(jnp.sum(jnp.where(hit, spread, 0.0), axis=0, keepdims=True))
        coef, through, before = [], [], []
        total = jnp.zeros((SUB, LANES), jnp.float32)
        for t in range(tiles):
            v = jnp.broadcast_to(picked[t * SUB : (t + 1) * SUB], (SUB, LANES))
            run = prefix(v) + total
            coef.append(v)
            through.append(run)
            before.append(run - v)
            total = last(run)
        return coef, through, before, total

    def terms():
        coef, through, before, total = depths()
        for j in range(width // LANES):
            at = pl.ds(j * LANES, LANES)
            r = jnp.broadcast_to(rate[0:1, at], (SUB, LANES))
            tail = jnp.zeros((SUB, LANES), jnp.float32)
            for t in reversed(range(tiles)):
                zs = pl.ds(t * SUB, SUB)
                rest = 1.0 - jnp.exp(-(coef[t] * r))
                inject[zs, at] = rest * jnp.exp(through[t] * r)
                h = rest * jnp.exp(-((through[t] + before[t]) * r))
                weigh[zs, at] = h
                lift = jnp.exp(before[t] * r)
                back[zs, at] = lift
                run = suffix(h) + tail
                reach[zs, at] = lift * run
                tail = first(run)
            early[d, 0, pl.ds(j, 1), :] = jnp.exp(-(total * r))[0:1]
            early[d, 1, pl.ds(j, 1), :] = tail[0:1]

    def prepare():
        for copy in copies[1:]:
            copy.wait()
        terms()

    turn = word.at[rounds + 1]
    copies = small_copies()

    @pl.when(c == 1)
    def _():
        prepare()
        pl.semaphore_wait(turn, 1)

    copies[0].wait()
    w_copy.wait_recv()

    def weight(ref):
        return 1.0 / jnp.full((SUB, LANES), ref[0]).astype(jnp.float32)

    w, v = weight(mine_count), weight(mate_count)

    def reduced(i, a, zs, at):
        at = pl.ds(i * width + at.start, at.size)
        if a == 0:
            return both[0, 0, zs, at] * w + both[1, 0, zs, at] * v
        return both[0, 1, zs, at] + both[1, 1, zs, at]

    def lanes(ch):
        return [pl.ds((chunks[ch][0] + j) * LANES, LANES) for j in range(chunks[ch][1])]

    for n, (i, ch) in enumerate(first_part):
        arrived(i, *chunks[ch][:2], got.at[n])
        for at in lanes(ch):
            for t in range(tiles):
                zs = pl.ds(t * SUB, SUB)
                for a in range(2):
                    sums[i - 1, a, zs, at] = reduced(i, a, zs, at)
        if ch in relays:
            pl.when(relayed(ch, d))(relay_copy(i, ch).start)
            pl.when(jnp.logical_not(relayed(ch, d)))(sums_copy(i, ch).start)
        else:
            sums_copy(i, ch).start()

    local = len(first_part)
    fetch(0, 0, width // LANES, got.at[local])
    give(0, 0, width // LANES, got.at[local])

    @pl.when(c == 0)
    def _():
        prepare()
        pl.semaphore_signal(turn, inc=1, device_id=(mate, d), device_id_type=MESH)

    for r in range(rounds):
        pass_on(r)
    for j in range(ks - 1):
        carry_copy(early, early_send, early_recv, j).start()

    arrived(0, 0, width // LANES, got.at[local])
    for n, ch in enumerate(taking):
        start, cols, _ = chunks[ch]
        wait_for(landed.at[:, :, :, columns(ch)], sums_recv.at[ch])
        for j, at in enumerate(lanes(ch)):
            carry = jnp.zeros((SUB, LANES), jnp.float32)
            parts = []
            for t in range(tiles):
                zs = pl.ds(t * SUB, SUB)
                num, den = reduced(0, 0, zs, at), reduced(0, 1, zs, at)
                for i in range(1, ys):
                    num = num + landed[i - 1, 0, zs, at]
                    den = den + landed[i - 1, 1, zs, at]
                run = prefix(inject[zs, at] * (num / den)) + carry
                parts.append(run)
                carry = last(run)
            row = pl.ds(start + j, 1)
            late[ch][d, pl.ds(j, 1), :] = carry[0:1] * early[d, 0, row, :]
            tail = jnp.zeros((SUB, LANES), jnp.float32)
            for t in reversed(range(tiles)):
                zs = pl.ds(t * SUB, SUB)
                run = suffix(weigh[zs, at] * parts[t]) + tail
                held[zs, at] = run
                tail = first(run)
            late[ch][d, pl.ds(cols + j, 1), :] = tail[0:1]
        for j in range(ks - 1):
            carry_copy(late[ch], late_send.at[ch], late_recv.at[ch], j).start()
        if n == 0:
            for r in relays:
                forward(r)

    others = pl.ds(0, ks - 1)
    wait_for(early.at[others], early_recv)
    for ch in taking:
        wait_for(late[ch].at[others], late_recv.at[ch])
        start, cols, _ = chunks[ch]
        rs = pl.ds(start, cols)
        down, lift = pl.ds(0, cols), pl.ds(cols, cols)
        state = jnp.zeros((cols, LANES), jnp.float32)
        mine = state
        ups = []
        for k in range(ks):
            mine = jnp.where(k == d, state, mine)
            ups.append(late[ch][k, lift] + early[k, 1, rs] * state)
            if k < ks - 1:
                state = late[ch][k, down] + early[k, 0, rs] * state
        up = jnp.zeros((cols, LANES), jnp.float32)
        for k in reversed(range(1, ks)):
            up = jnp.where(k > d, ups[k] + early[k, 0, rs] * up, up)
        states[0, rs] = mine
        states[1, rs] = up * early[d, 0, rs]
        for j, at in enumerate(lanes(ch)):
            row = pl.ds(start + j, 1)
            e = jnp.broadcast_to(states[0, row, :], (SUB, LANES))
            b = jnp.broadcast_to(states[1, row, :], (SUB, LANES))
            for t in range(tiles):
                zs = pl.ds(t * SUB, SUB)
                out[zs, at] = back[zs, at] * (held[zs, at] + b) + reach[zs, at] * e

    w_copy.wait_send()
    wait_for(both.at[1], part_send)
    wait_for(sums, sums_send)
    for ch in relays:
        pl.when(relayed(ch, d + stride(ch)))(
            functools.partial(wait_for, via[ch], via_send.at[relays.index(ch)])
        )
    wait_for(early.at[others], early_send)
    for ch in taking:
        wait_for(late[ch].at[others], late_send.at[ch])


def split(blocks, ys, ks):
    edge = max(1, blocks // 8)
    hops = RELAYS if ys == 2 and ks >= 6 and blocks >= 16 else ()
    inner = blocks - 2 * edge - sum(n for n, _ in hops)
    sizes = [edge, *(n for n, _ in hops), inner - inner // 2, inner // 2, edge]
    ways = [None, *(way for _, way in hops), None, None, None]
    found = [(sum(sizes[:n]), size, ways[n]) for n, size in enumerate(sizes)]
    detours = range(1, len(hops) + 1)
    straight = range(len(hops) + 1, len(found) - 1)
    return found, range(len(found)), [0, *straight, *detours, len(found) - 1]


def shards(ys, ks, grad_part, illum_part, source_count, rate, coef_table, coef_index):
    _, rows, lateral = grad_part.shape
    width = lateral // (2 * ys)
    blocks = width // LANES
    chunks, sending, taking = split(blocks, ys, ks)
    relays = [chunk for chunk in chunks if chunk[2]]
    f32, i32 = jnp.float32, jnp.int32
    dma = pltpu.SemaphoreType.DMA
    sent = pltpu.VMEM((ys - 1, 2, rows, width), f32)
    field = pltpu.VMEM((rows, width), f32)
    anywhere = pl.BlockSpec(memory_space=pl.ANY)
    small = (rate.reshape(1, -1), coef_table.reshape(1, -1), coef_index.reshape(1, -1))
    return pl.pallas_call(
        functools.partial(body, (ys, ks, rows, width, chunks, sending, taking)),
        out_shape=jax.ShapeDtypeStruct((rows, width), f32),
        in_specs=[anywhere] * 6,
        out_specs=pl.BlockSpec(memory_space=pltpu.VMEM),
        scratch_shapes=[
            pltpu.VMEM((2, 2, rows, ys * width), f32),
            sent,
            sent,
            pltpu.VMEM((ks, 2, blocks, LANES), f32),
            field, field, field, field, field,
            pltpu.VMEM((2, blocks, LANES), f32),
            pltpu.VMEM(small[0].shape, f32),
            pltpu.VMEM(small[1].shape, f32),
            pltpu.VMEM(small[2].shape, i32),
            pltpu.SMEM((1,), i32),
            pltpu.SMEM((1,), i32),
            *[pltpu.VMEM((ks, 2 * n, LANES), f32) for _, n, _ in chunks],
            *[pltpu.VMEM((ys - 1, 2, rows, n * LANES), f32) for _, n, _ in relays],
            dma(((ys - 1) * len(chunks) + 1,)),
            dma,
            dma,
            dma((len(chunks),)),
            dma((max(1, len(relays)),)),
            dma((max(1, len(relays)),)),
            dma,
            dma,
            dma((len(chunks),)),
            dma((len(chunks),)),
            dma,
            dma,
            dma((4,)),
            pltpu.SemaphoreType.REGULAR((ks // 2 + 2,)),
        ],
        compiler_params=pltpu.CompilerParams(collective_id=0, has_side_effects=True, vmem_limit_bytes=53 * 2**20),
    )(
        grad_part,
        illum_part,
        source_count,
        *[pltpu.with_memory_space_constraint(x, pltpu.HBM) for x in small],
    )


def solution(mesh):
    placed = (
        P("shot", "depth", None),
        P("shot", "depth", None),
        P("shot"),
        P("shot"),
        P(),
        P("depth"),
    )
    return jax.shard_map(
        functools.partial(shards, mesh.shape["shot"] // 2, mesh.shape["depth"]),
        mesh=mesh, in_specs=placed, out_specs=P("depth", "shot"), check_vma=False,
    )
```

```python
import functools

import jax
import jax.numpy as jnp
from jax import lax
from jax.experimental import pallas as pl
from jax.experimental.pallas import tpu as pltpu
from jax.sharding import PartitionSpec as P

MESH = pl.DeviceIdType.MESH
LANES = 128
SUB = 8


def deep(at, ks):
    return (at >= 2) & (at < ks)


def middle(at, ks):
    return (at >= 2) & (at < ks - 2)


def odd(at, ks):
    return lax.rem(at, 2) == 1


ROUTES = ((2, deep), (1, odd))
RELAYS = ((2, (2, deep)), (1, (2, middle)), (1, (1, odd)))


def body(
    dims,
    grad, illum, count, rate_hbm, table_hbm, index_hbm, out,
    both, sums, landed, early, inject, weigh, back, reach, held, states,
    rate, table, index, mate_count, *rest,
):
    ys, ks, rows, width, chunks, loads, turns = dims
    relays = [ch for ch in range(len(chunks)) if chunks[ch][2]]
    late, rest = rest[: len(turns)], rest[len(turns) :]
    via, rest = dict(zip(relays, rest)), rest[len(relays) :]
    (
        got, part_send, sums_send, sums_recv, via_recv, via_send,
        early_send, early_recv, late_send, late_recv, w_send, w_recv, small_sem, word,
    ) = rest
    tiles = rows // SUB
    me = lax.axis_index("shot")
    d = lax.axis_index("depth")
    y, c = me // 2, me % 2
    mate = y * 2 + 1 - c

    def peer(j):
        return j + (d <= j).astype(jnp.int32)

    def other(i):
        return lax.rem(y + i, ys)

    def greet(semaphore):
        flip = d + 1 - 2 * lax.rem(d, 2)
        pl.semaphore_signal(semaphore, inc=1, device_id=(me, flip), device_id_type=MESH)
        for step in (2, -2):
            near = d + step

            @pl.when((near >= 0) & (near < ks))
            def _():
                pl.semaphore_signal(semaphore, inc=1, device_id=(me, near), device_id_type=MESH)

    def neighbours():
        return (d >= 2).astype(jnp.int32) + (d < ks - 2).astype(jnp.int32) + 1

    def relayed(ch, at):
        return chunks[ch][2][1](at, ks)

    def stride(ch):
        return chunks[ch][2][0]

    barrier = pltpu.get_barrier_semaphore()
    pl.semaphore_signal(barrier, inc=1, device_id=(mate, d), device_id_type=MESH)
    for i in range(1, ys):
        pl.semaphore_signal(barrier, inc=1, device_id=(other(i) * 2 + c, d), device_id_type=MESH)
    pl.when(y == 0)(functools.partial(greet, barrier))
    expected = ys + (y == 0).astype(jnp.int32) * neighbours()
    for step, some in ROUTES if relays else ():
        expected = expected + some(d, ks).astype(jnp.int32) * (ys - 1)

        @pl.when(some(d + step, ks))
        def _():
            for i in range(1, ys):
                pl.semaphore_signal(barrier, inc=1, device_id=(other(i) * 2 + c, d + step), device_id_type=MESH)

    def reach_of(group):
        return chunks[group[0]][0], sum(chunks[ch][1] for ch in group)

    def columns(ch):
        return pl.ds(chunks[ch][0] * LANES, chunks[ch][1] * LANES)

    def fetch(i, start, cols, semaphore):
        into = pl.ds(i * width + start * LANES, cols * LANES)
        for a, src in enumerate((grad, illum)):
            at = pl.multiple_of((other(i) * 2 + c) * width + start * LANES, LANES)
            pltpu.make_async_copy(
                src.at[0, :, pl.ds(at, cols * LANES)], both.at[0, a, :, into], semaphore
            ).start()

    def give(i, start, cols, semaphore):
        into = pl.ds(i * width + start * LANES, cols * LANES)
        for a, src in enumerate((grad, illum)):
            at = pl.multiple_of((other(i) * 2 + 1 - c) * width + start * LANES, LANES)
            pltpu.make_async_remote_copy(
                src_ref=src.at[0, :, pl.ds(at, cols * LANES)],
                dst_ref=both.at[1, a, :, into],
                send_sem=part_send,
                recv_sem=semaphore,
                device_id=(mate, d),
                device_id_type=MESH,
            ).start()

    def wait_for(ref, semaphore):
        pltpu.make_async_copy(ref, ref, semaphore).wait()

    def arrived(i, start, cols, semaphore):
        wait_for(both.at[:, :, :, pl.ds(i * width + start * LANES, cols * LANES)], semaphore)

    def sums_copy(i, ch):
        return pltpu.make_async_remote_copy(
            src_ref=sums.at[i - 1, :, :, columns(ch)],
            dst_ref=landed.at[i - 1, :, :, columns(ch)],
            send_sem=sums_send,
            recv_sem=sums_recv.at[ch],
            device_id=(other(i) * 2 + c, d),
            device_id_type=MESH,
        )

    def relay_copy(i, ch):
        return pltpu.make_async_remote_copy(
            src_ref=sums.at[i - 1, :, :, columns(ch)],
            dst_ref=via[ch].at[i - 1],
            send_sem=sums_send,
            recv_sem=via_recv.at[relays.index(ch)],
            device_id=(other(i) * 2 + c, d - stride(ch)),
            device_id_type=MESH,
        )

    def forward(ch):
        @pl.when(relayed(ch, d + stride(ch)))
        def _():
            wait_for(via[ch], via_recv.at[relays.index(ch)])
            for i in range(1, ys):
                pltpu.make_async_remote_copy(
                    src_ref=via[ch].at[i - 1],
                    dst_ref=landed.at[i - 1, :, :, columns(ch)],
                    send_sem=via_send.at[relays.index(ch)],
                    recv_sem=sums_recv.at[ch],
                    device_id=(me, d + stride(ch)),
                    device_id_type=MESH,
                ).start()

    def carry_copy(buffer, send, recv, j):
        return pltpu.make_async_remote_copy(
            src_ref=buffer.at[d],
            dst_ref=buffer.at[d],
            send_sem=send,
            recv_sem=recv,
            device_id=(me, peer(j)),
            device_id_type=MESH,
        )

    w_copy = pltpu.make_async_remote_copy(
        src_ref=count,
        dst_ref=mate_count,
        send_sem=w_send,
        recv_sem=w_recv,
        device_id=(mate, d),
        device_id_type=MESH,
    )

    def small_copies():
        pairs = ((table_hbm, table), (index_hbm, index), (rate_hbm, rate))
        return [pltpu.make_async_copy(a, b, small_sem.at[n]) for n, (a, b) in enumerate(pairs)]

    first_part = [(i, group) for group in loads for i in range(1, ys)]
    fetch(1, *reach_of(loads[0]), got.at[0])

    pl.semaphore_wait(barrier, expected)
    w_copy.start()
    for n, (i, group) in enumerate(first_part):
        give(i, *reach_of(group), got.at[n])
    for n, (i, group) in enumerate(first_part[1:], 1):
        fetch(i, *reach_of(group), got.at[n])
    for copy in small_copies():
        copy.start()

    rounds = ks // 2
    pl.when(y == 0)(functools.partial(greet, word.at[0]))

    def pass_on(r):
        @pl.when(y == 0)
        def _():
            pl.semaphore_wait(word.at[r], neighbours())
            if r + 1 < rounds:
                greet(word.at[r + 1])
            else:
                for i in range(1, ys):
                    pl.semaphore_signal(
                        word.at[rounds], inc=1, device_id=(other(i) * 2 + c, d), device_id_type=MESH
                    )

        if r + 1 == rounds:
            pl.when(y != 0)(lambda: pl.semaphore_wait(word.at[rounds], 1))

    sub = lax.broadcasted_iota(jnp.int32, (SUB, LANES), 0)

    def prefix(v):
        for s in (1, 2, 4):
            v = v + jnp.where(sub >= s, pltpu.roll(v, s, 0), 0.0)
        return v

    def suffix(v):
        for s in (1, 2, 4):
            v = v + jnp.where(sub < SUB - s, pltpu.roll(v, SUB - s, 0), 0.0)
        return v

    def first(v):
        return jnp.broadcast_to(v[0:1], (SUB, LANES))

    def last(v):
        return jnp.broadcast_to(v[SUB - 1 : SUB], (SUB, LANES))

    entries = table.shape[1]

    def upright(row):
        n = row.shape[1]
        diagonal = lax.broadcasted_iota(jnp.int32, (n, n), 0) == lax.broadcasted_iota(
            jnp.int32, (n, n), 1
        )
        return jnp.sum(
            jnp.where(diagonal, jnp.broadcast_to(row, (n, n)), 0.0), axis=1, keepdims=True
        )

    def depths():
        level = lax.broadcasted_iota(jnp.int32, (entries, rows), 0)
        hit = jnp.broadcast_to(index[...], (entries, rows)) == level
        spread = jnp.broadcast_to(upright(table[...]), (entries, rows))
        picked = upright(jnp.sum(jnp.where(hit, spread, 0.0), axis=0, keepdims=True))
        coef, through, before = [], [], []
        total = jnp.zeros((SUB, LANES), jnp.float32)
        for t in range(tiles):
            v = jnp.broadcast_to(picked[t * SUB : (t + 1) * SUB], (SUB, LANES))
            run = prefix(v) + total
            coef.append(v)
            through.append(run)
            before.append(run - v)
            total = last(run)
        return coef, through, before, total

    def terms():
        coef, through, before, total = depths()
        for j in range(width // LANES):
            at = pl.ds(j * LANES, LANES)
            r = jnp.broadcast_to(rate[0:1, at], (SUB, LANES))
            tail = jnp.zeros((SUB, LANES), jnp.float32)
            for t in reversed(range(tiles)):
                zs = pl.ds(t * SUB, SUB)
                rest = 1.0 - jnp.exp(-(coef[t] * r))
                inject[zs, at] = rest * jnp.exp(through[t] * r)
                h = rest * jnp.exp(-((through[t] + before[t]) * r))
                weigh[zs, at] = h
                lift = jnp.exp(before[t] * r)
                back[zs, at] = lift
                run = suffix(h) + tail
                reach[zs, at] = lift * run
                tail = first(run)
            early[d, 0, pl.ds(j, 1), :] = jnp.exp(-(total * r))[0:1]
            early[d, 1, pl.ds(j, 1), :] = tail[0:1]

    def prepare():
        for copy in small_copies():
            copy.wait()
        terms()

    turn = word.at[rounds + 1]

    @pl.when(c == 1)
    def _():
        prepare()
        pl.semaphore_wait(turn, 1)

    w_copy.wait_recv()

    def weight(ref):
        return 1.0 / jnp.full((SUB, LANES), ref[0]).astype(jnp.float32)

    w, v = weight(count), weight(mate_count)

    def reduced(i, a, zs, at):
        at = pl.ds(i * width + at.start, at.size)
        if a == 0:
            return both[0, 0, zs, at] * w + both[1, 0, zs, at] * v
        return both[0, 1, zs, at] + both[1, 1, zs, at]

    def lanes(start, cols):
        return [pl.ds((start + j) * LANES, LANES) for j in range(cols)]

    for n, (i, group) in enumerate(first_part):
        arrived(i, *reach_of(group), got.at[n])
        for ch in group:
            for at in lanes(*chunks[ch][:2]):
                for t in range(tiles):
                    zs = pl.ds(t * SUB, SUB)
                    for a in range(2):
                        sums[i - 1, a, zs, at] = reduced(i, a, zs, at)
            if ch in relays:
                pl.when(relayed(ch, d))(relay_copy(i, ch).start)
                pl.when(jnp.logical_not(relayed(ch, d)))(sums_copy(i, ch).start)
            else:
                sums_copy(i, ch).start()

    local = len(first_part)
    fetch(0, 0, width // LANES, got.at[local])
    give(0, 0, width // LANES, got.at[local])

    @pl.when(c == 0)
    def _():
        prepare()
        pl.semaphore_signal(turn, inc=1, device_id=(mate, d), device_id_type=MESH)

    for r in range(rounds):
        pass_on(r)
    for j in range(ks - 1):
        carry_copy(early, early_send, early_recv, j).start()

    arrived(0, 0, width // LANES, got.at[local])
    for n, group in enumerate(turns):
        start, cols = reach_of(group)
        for ch in group:
            wait_for(landed.at[:, :, :, columns(ch)], sums_recv.at[ch])
        for j, at in enumerate(lanes(start, cols)):
            carry = jnp.zeros((SUB, LANES), jnp.float32)
            parts = []
            for t in range(tiles):
                zs = pl.ds(t * SUB, SUB)
                num, den = reduced(0, 0, zs, at), reduced(0, 1, zs, at)
                for i in range(1, ys):
                    num = num + landed[i - 1, 0, zs, at]
                    den = den + landed[i - 1, 1, zs, at]
                run = prefix(inject[zs, at] * (num / den)) + carry
                parts.append(run)
                carry = last(run)
            row = pl.ds(start + j, 1)
            late[n][d, pl.ds(j, 1), :] = carry[0:1] * early[d, 0, row, :]
            tail = jnp.zeros((SUB, LANES), jnp.float32)
            for t in reversed(range(tiles)):
                zs = pl.ds(t * SUB, SUB)
                run = suffix(weigh[zs, at] * parts[t]) + tail
                held[zs, at] = run
                tail = first(run)
            late[n][d, pl.ds(cols + j, 1), :] = tail[0:1]
        for j in range(ks - 1):
            carry_copy(late[n], late_send, late_recv.at[n], j).start()
        if n == 0:
            for r in relays:
                forward(r)

    others = pl.ds(0, ks - 1)
    wait_for(early.at[others], early_recv)
    for n, group in enumerate(turns):
        wait_for(late[n].at[others], late_recv.at[n])
        start, cols = reach_of(group)
        rs = pl.ds(start, cols)
        down, lift = pl.ds(0, cols), pl.ds(cols, cols)
        state = jnp.zeros((cols, LANES), jnp.float32)
        mine = state
        ups = []
        for k in range(ks):
            mine = jnp.where(k == d, state, mine)
            ups.append(late[n][k, lift] + early[k, 1, rs] * state)
            if k < ks - 1:
                state = late[n][k, down] + early[k, 0, rs] * state
        up = jnp.zeros((cols, LANES), jnp.float32)
        for k in reversed(range(1, ks)):
            up = jnp.where(k > d, ups[k] + early[k, 0, rs] * up, up)
        states[0, rs] = mine
        states[1, rs] = up * early[d, 0, rs]
        for j, at in enumerate(lanes(start, cols)):
            row = pl.ds(start + j, 1)
            e = jnp.broadcast_to(states[0, row, :], (SUB, LANES))
            b = jnp.broadcast_to(states[1, row, :], (SUB, LANES))
            for t in range(tiles):
                zs = pl.ds(t * SUB, SUB)
                out[zs, at] = back[zs, at] * (held[zs, at] + b) + reach[zs, at] * e

    w_copy.wait_send()
    wait_for(both.at[1], part_send)
    wait_for(sums, sums_send)
    for ch in relays:
        pl.when(relayed(ch, d + stride(ch)))(
            functools.partial(wait_for, via[ch], via_send.at[relays.index(ch)])
        )
    wait_for(early.at[others], early_send)
    wait_for(early.at[others], late_send)


def split(blocks, ys, ks):
    edge = max(1, blocks // 8)
    hops = RELAYS if ys == 2 and ks >= 6 and blocks >= 16 else ()
    inner = blocks - 2 * edge - sum(n for n, _ in hops)
    sizes = [max(1, edge // 2), *(n for n, _ in hops), inner - inner // 2, inner // 2 + edge - max(1, edge // 2), edge]
    ways = [None, *(way for _, way in hops), None, None, None]
    found = [(sum(sizes[:n]), size, ways[n]) for n, size in enumerate(sizes)]
    n = len(hops) + 1
    detours = [tuple(range(1, n))] if hops else []
    return found, [(0,), *detours, (n, n + 1, n + 2)], [(0,), (n,), (n + 1,), *[(m,) for m in range(1, n)], (n + 2,)]


def shards(ys, ks, grad_part, illum_part, source_count, rate, coef_table, coef_index):
    _, rows, lateral = grad_part.shape
    width = lateral // (2 * ys)
    blocks = width // LANES
    chunks, loads, turns = split(blocks, ys, ks)
    relays = [chunk for chunk in chunks if chunk[2]]
    f32, i32 = jnp.float32, jnp.int32
    dma = pltpu.SemaphoreType.DMA
    sent = pltpu.VMEM((ys - 1, 2, rows, width), f32)
    field = pltpu.VMEM((rows, width), f32)
    anywhere = pl.BlockSpec(memory_space=pl.ANY)
    small = (rate.reshape(1, -1), coef_table.reshape(1, -1), coef_index.reshape(1, -1))
    return pl.pallas_call(
        functools.partial(body, (ys, ks, rows, width, chunks, loads, turns)),
        out_shape=jax.ShapeDtypeStruct((rows, width), f32),
        in_specs=[anywhere] * 2 + [pl.BlockSpec(memory_space=pltpu.SMEM)] + [anywhere] * 3,
        out_specs=pl.BlockSpec(memory_space=pltpu.VMEM),
        scratch_shapes=[
            pltpu.VMEM((2, 2, rows, ys * width), f32),
            sent,
            sent,
            pltpu.VMEM((ks, 2, blocks, LANES), f32),
            field, field, field, field, field,
            pltpu.VMEM((2, blocks, LANES), f32),
            pltpu.VMEM(small[0].shape, f32),
            pltpu.VMEM(small[1].shape, f32),
            pltpu.VMEM(small[2].shape, i32),
            pltpu.SMEM((1,), i32),
            *[pltpu.VMEM((ks, 2 * sum(chunks[ch][1] for ch in group), LANES), f32) for group in turns],
            *[pltpu.VMEM((ys - 1, 2, rows, n * LANES), f32) for _, n, _ in relays],
            dma(((ys - 1) * len(loads) + 1,)),
            dma,
            dma,
            dma((len(chunks),)),
            dma((max(1, len(relays)),)),
            dma((max(1, len(relays)),)),
            dma,
            dma,
            dma,
            dma((len(turns),)),
            dma,
            dma,
            dma((3,)),
            pltpu.SemaphoreType.REGULAR((ks // 2 + 2,)),
        ],
        compiler_params=pltpu.CompilerParams(collective_id=0, has_side_effects=True, vmem_limit_bytes=53 * 2**20),
    )(
        grad_part,
        illum_part,
        source_count,
        *[pltpu.with_memory_space_constraint(x, pltpu.HBM) for x in small],
    )


def solution(mesh):
    placed = (
        P("shot", "depth", None),
        P("shot", "depth", None),
        P("shot"),
        P("shot"),
        P(),
        P("depth"),
    )
    return jax.shard_map(
        functools.partial(shards, mesh.shape["shot"] // 2, mesh.shape["depth"]),
        mesh=mesh, in_specs=placed, out_specs=P("depth", "shot"), check_vma=False,
    )
```

```python
import functools

import jax
import jax.numpy as jnp
from jax import lax
from jax.experimental import pallas as pl
from jax.experimental.pallas import tpu as pltpu
from jax.sharding import PartitionSpec as P

MESH = pl.DeviceIdType.MESH
LANES = 128
SUB = 8


def deep(at, ks):
    return (at >= 2) & (at < ks)


def middle(at, ks):
    return (at >= 2) & (at < ks - 2)


def odd(at, ks):
    return lax.rem(at, 2) == 1


ROUTES = ((2, deep), (1, odd))
RELAYS = ((2, (2, deep)), (1, (2, middle)), (1, (1, odd)))


def body(
    dims,
    grad, illum, count, rate_hbm, table_hbm, index_hbm, out,
    both, sums, landed, early, inject, weigh, back, reach, held, states,
    rate, table, index, mate_count, *rest,
):
    ys, ks, rows, width, chunks, loads, turns = dims
    relays = [ch for ch in range(len(chunks)) if chunks[ch][2]]
    late, rest = rest[: len(turns)], rest[len(turns) :]
    via, rest = dict(zip(relays, rest)), rest[len(relays) :]
    (
        got, part_send, sums_send, sums_recv, via_recv, via_send,
        early_send, early_recv, late_send, late_recv, w_send, w_recv, small_sem, word,
    ) = rest
    tiles = rows // SUB
    me = lax.axis_index("shot")
    d = lax.axis_index("depth")
    y, c = me // 2, me % 2
    mate = y * 2 + 1 - c

    def peer(j):
        return j + (d <= j).astype(jnp.int32)

    def other(i):
        return lax.rem(y + i, ys)

    def greet(semaphore):
        flip = d + 1 - 2 * lax.rem(d, 2)
        pl.semaphore_signal(semaphore, inc=1, device_id=(me, flip), device_id_type=MESH)
        for step in (2, -2):
            near = d + step

            @pl.when((near >= 0) & (near < ks))
            def _():
                pl.semaphore_signal(semaphore, inc=1, device_id=(me, near), device_id_type=MESH)

    def neighbours():
        return (d >= 2).astype(jnp.int32) + (d < ks - 2).astype(jnp.int32) + 1

    def relayed(ch, at):
        return chunks[ch][2][1](at, ks)

    def stride(ch):
        return chunks[ch][2][0]

    barrier = pltpu.get_barrier_semaphore()
    pl.semaphore_signal(barrier, inc=1, device_id=(mate, d), device_id_type=MESH)
    for i in range(1, ys):
        pl.semaphore_signal(barrier, inc=1, device_id=(other(i) * 2 + c, d), device_id_type=MESH)
    pl.when(y == 0)(functools.partial(greet, barrier))
    expected = ys + (y == 0).astype(jnp.int32) * neighbours()
    for step, some in ROUTES if relays else ():
        expected = expected + some(d, ks).astype(jnp.int32) * (ys - 1)

        @pl.when((c == 1) & some(d + step, ks))
        def _():
            for i in range(1, ys):
                for own in range(2):
                    pl.semaphore_signal(
                        barrier, inc=1, device_id=(other(i) * 2 + own, d + step), device_id_type=MESH
                    )

    def reach_of(group):
        return chunks[group[0]][0], sum(chunks[ch][1] for ch in group)

    def columns(ch):
        return pl.ds(chunks[ch][0] * LANES, chunks[ch][1] * LANES)

    def fetch(i, start, cols, semaphore):
        into = pl.ds(i * width + start * LANES, cols * LANES)
        for a, src in enumerate((grad, illum)):
            at = pl.multiple_of((other(i) * 2 + c) * width + start * LANES, LANES)
            pltpu.make_async_copy(
                src.at[0, :, pl.ds(at, cols * LANES)], both.at[0, a, :, into], semaphore
            ).start()

    def give(i, start, cols, semaphore):
        into = pl.ds(i * width + start * LANES, cols * LANES)
        for a, src in enumerate((grad, illum)):
            at = pl.multiple_of((other(i) * 2 + 1 - c) * width + start * LANES, LANES)
            pltpu.make_async_remote_copy(
                src_ref=src.at[0, :, pl.ds(at, cols * LANES)],
                dst_ref=both.at[1, a, :, into],
                send_sem=part_send,
                recv_sem=semaphore,
                device_id=(mate, d),
                device_id_type=MESH,
            ).start()

    def wait_for(ref, semaphore):
        pltpu.make_async_copy(ref, ref, semaphore).wait()

    def arrived(i, start, cols, semaphore):
        wait_for(both.at[:, :, :, pl.ds(i * width + start * LANES, cols * LANES)], semaphore)

    def sums_copy(i, ch):
        return pltpu.make_async_remote_copy(
            src_ref=sums.at[i - 1, :, :, columns(ch)],
            dst_ref=landed.at[i - 1, :, :, columns(ch)],
            send_sem=sums_send,
            recv_sem=sums_recv.at[ch],
            device_id=(other(i) * 2 + c, d),
            device_id_type=MESH,
        )

    def relay_copy(i, ch):
        return pltpu.make_async_remote_copy(
            src_ref=sums.at[i - 1, :, :, columns(ch)],
            dst_ref=via[ch].at[c, i - 1],
            send_sem=sums_send,
            recv_sem=via_recv.at[c, relays.index(ch)],
            device_id=(other(i) * 2 + 1, d - stride(ch)),
            device_id_type=MESH,
        )

    def forwards(ch):
        return (c == 1) & relayed(ch, d + stride(ch))

    def forward(ch):
        @pl.when(forwards(ch))
        def _():
            for own in range(2):
                wait_for(via[ch].at[own], via_recv.at[own, relays.index(ch)])
                for i in range(1, ys):
                    pltpu.make_async_remote_copy(
                        src_ref=via[ch].at[own, i - 1],
                        dst_ref=landed.at[i - 1, :, :, columns(ch)],
                        send_sem=via_send.at[relays.index(ch)],
                        recv_sem=sums_recv.at[ch],
                        device_id=(y * 2 + own, d + stride(ch)),
                        device_id_type=MESH,
                    ).start()

    def carry_copy(buffer, send, recv, j):
        return pltpu.make_async_remote_copy(
            src_ref=buffer.at[d],
            dst_ref=buffer.at[d],
            send_sem=send,
            recv_sem=recv,
            device_id=(me, peer(j)),
            device_id_type=MESH,
        )

    w_copy = pltpu.make_async_remote_copy(
        src_ref=count,
        dst_ref=mate_count,
        send_sem=w_send,
        recv_sem=w_recv,
        device_id=(mate, d),
        device_id_type=MESH,
    )

    def small_copies():
        pairs = ((table_hbm, table), (index_hbm, index), (rate_hbm, rate))
        return [pltpu.make_async_copy(a, b, small_sem.at[n]) for n, (a, b) in enumerate(pairs)]

    first_part = [(i, group) for group in loads for i in range(1, ys)]
    fetch(1, *reach_of(loads[0]), got.at[0])

    pl.semaphore_wait(barrier, expected)
    w_copy.start()
    for n, (i, group) in enumerate(first_part):
        give(i, *reach_of(group), got.at[n])
    for n, (i, group) in enumerate(first_part[1:], 1):
        fetch(i, *reach_of(group), got.at[n])
    for copy in small_copies():
        copy.start()

    rounds = ks // 2
    pl.when(y == 0)(functools.partial(greet, word.at[0]))

    def pass_on(r):
        @pl.when(y == 0)
        def _():
            pl.semaphore_wait(word.at[r], neighbours())
            if r + 1 < rounds:
                greet(word.at[r + 1])
            else:
                for i in range(1, ys):
                    pl.semaphore_signal(
                        word.at[rounds], inc=1, device_id=(other(i) * 2 + c, d), device_id_type=MESH
                    )

        if r + 1 == rounds:
            pl.when(y != 0)(lambda: pl.semaphore_wait(word.at[rounds], 1))

    sub = lax.broadcasted_iota(jnp.int32, (SUB, LANES), 0)

    def prefix(v):
        for s in (1, 2, 4):
            v = v + jnp.where(sub >= s, pltpu.roll(v, s, 0), 0.0)
        return v

    def suffix(v):
        for s in (1, 2, 4):
            v = v + jnp.where(sub < SUB - s, pltpu.roll(v, SUB - s, 0), 0.0)
        return v

    def first(v):
        return jnp.broadcast_to(v[0:1], (SUB, LANES))

    def last(v):
        return jnp.broadcast_to(v[SUB - 1 : SUB], (SUB, LANES))

    entries = table.shape[1]

    def upright(row):
        n = row.shape[1]
        diagonal = lax.broadcasted_iota(jnp.int32, (n, n), 0) == lax.broadcasted_iota(
            jnp.int32, (n, n), 1
        )
        return jnp.sum(
            jnp.where(diagonal, jnp.broadcast_to(row, (n, n)), 0.0), axis=1, keepdims=True
        )

    def depths():
        level = lax.broadcasted_iota(jnp.int32, (entries, rows), 0)
        hit = jnp.broadcast_to(index[...], (entries, rows)) == level
        spread = jnp.broadcast_to(upright(table[...]), (entries, rows))
        picked = upright(jnp.sum(jnp.where(hit, spread, 0.0), axis=0, keepdims=True))
        coef, through, before = [], [], []
        total = jnp.zeros((SUB, LANES), jnp.float32)
        for t in range(tiles):
            v = jnp.broadcast_to(picked[t * SUB : (t + 1) * SUB], (SUB, LANES))
            run = prefix(v) + total
            coef.append(v)
            through.append(run)
            before.append(run - v)
            total = last(run)
        return coef, through, before, total

    def terms():
        coef, through, before, total = depths()
        for j in range(width // LANES):
            at = pl.ds(j * LANES, LANES)
            r = jnp.broadcast_to(rate[0:1, at], (SUB, LANES))
            tail = jnp.zeros((SUB, LANES), jnp.float32)
            for t in reversed(range(tiles)):
                zs = pl.ds(t * SUB, SUB)
                rest = 1.0 - jnp.exp(-(coef[t] * r))
                inject[zs, at] = rest * jnp.exp(through[t] * r)
                h = rest * jnp.exp(-((through[t] + before[t]) * r))
                weigh[zs, at] = h
                lift = jnp.exp(before[t] * r)
                back[zs, at] = lift
                run = suffix(h) + tail
                reach[zs, at] = lift * run
                tail = first(run)
            early[d, 0, pl.ds(j, 1), :] = jnp.exp(-(total * r))[0:1]
            early[d, 1, pl.ds(j, 1), :] = tail[0:1]

    def prepare():
        for copy in small_copies():
            copy.wait()
        terms()

    turn = word.at[rounds + 1]

    @pl.when(c == 1)
    def _():
        prepare()
        pl.semaphore_wait(turn, 1)

    w_copy.wait_recv()

    def weight(ref):
        return 1.0 / jnp.full((SUB, LANES), ref[0]).astype(jnp.float32)

    w, v = weight(count), weight(mate_count)

    def reduced(i, a, zs, at):
        at = pl.ds(i * width + at.start, at.size)
        if a == 0:
            return both[0, 0, zs, at] * w + both[1, 0, zs, at] * v
        return both[0, 1, zs, at] + both[1, 1, zs, at]

    def lanes(start, cols):
        return [pl.ds((start + j) * LANES, LANES) for j in range(cols)]

    for n, (i, group) in enumerate(first_part):
        arrived(i, *reach_of(group), got.at[n])
        for ch in group:
            for at in lanes(*chunks[ch][:2]):
                for t in range(tiles):
                    zs = pl.ds(t * SUB, SUB)
                    for a in range(2):
                        sums[i - 1, a, zs, at] = reduced(i, a, zs, at)
            if ch in relays:
                pl.when(relayed(ch, d))(relay_copy(i, ch).start)
                pl.when(jnp.logical_not(relayed(ch, d)))(sums_copy(i, ch).start)
            else:
                sums_copy(i, ch).start()

    local = len(first_part)
    fetch(0, 0, width // LANES, got.at[local])
    give(0, 0, width // LANES, got.at[local])

    @pl.when(c == 0)
    def _():
        prepare()
        pl.semaphore_signal(turn, inc=1, device_id=(mate, d), device_id_type=MESH)

    for r in range(rounds):
        pass_on(r)
    for r in relays:
        forward(r)
    for j in range(ks - 1):
        carry_copy(early, early_send, early_recv, j).start()

    arrived(0, 0, width // LANES, got.at[local])
    for n, group in enumerate(turns):
        start, cols = reach_of(group)
        for ch in group:
            wait_for(landed.at[:, :, :, columns(ch)], sums_recv.at[ch])
        for j, at in enumerate(lanes(start, cols)):
            carry = jnp.zeros((SUB, LANES), jnp.float32)
            parts = []
            for t in range(tiles):
                zs = pl.ds(t * SUB, SUB)
                num, den = reduced(0, 0, zs, at), reduced(0, 1, zs, at)
                for i in range(1, ys):
                    num = num + landed[i - 1, 0, zs, at]
                    den = den + landed[i - 1, 1, zs, at]
                run = prefix(inject[zs, at] * (num / den)) + carry
                parts.append(run)
                carry = last(run)
            row = pl.ds(start + j, 1)
            late[n][d, pl.ds(j, 1), :] = carry[0:1] * early[d, 0, row, :]
            tail = jnp.zeros((SUB, LANES), jnp.float32)
            for t in reversed(range(tiles)):
                zs = pl.ds(t * SUB, SUB)
                run = suffix(weigh[zs, at] * parts[t]) + tail
                held[zs, at] = run
                tail = first(run)
            late[n][d, pl.ds(cols + j, 1), :] = tail[0:1]
        for j in range(ks - 1):
            carry_copy(late[n], late_send, late_recv.at[n], j).start()

    others = pl.ds(0, ks - 1)
    wait_for(early.at[others], early_recv)
    for n, group in enumerate(turns):
        wait_for(late[n].at[others], late_recv.at[n])
        start, cols = reach_of(group)
        rs = pl.ds(start, cols)
        down, lift = pl.ds(0, cols), pl.ds(cols, cols)
        state = jnp.zeros((cols, LANES), jnp.float32)
        mine = state
        ups = []
        for k in range(ks):
            mine = jnp.where(k == d, state, mine)
            ups.append(late[n][k, lift] + early[k, 1, rs] * state)
            if k < ks - 1:
                state = late[n][k, down] + early[k, 0, rs] * state
        up = jnp.zeros((cols, LANES), jnp.float32)
        for k in reversed(range(1, ks)):
            up = jnp.where(k > d, ups[k] + early[k, 0, rs] * up, up)
        states[0, rs] = mine
        states[1, rs] = up * early[d, 0, rs]
        for j, at in enumerate(lanes(start, cols)):
            row = pl.ds(start + j, 1)
            e = jnp.broadcast_to(states[0, row, :], (SUB, LANES))
            b = jnp.broadcast_to(states[1, row, :], (SUB, LANES))
            for t in range(tiles):
                zs = pl.ds(t * SUB, SUB)
                out[zs, at] = back[zs, at] * (held[zs, at] + b) + reach[zs, at] * e

    w_copy.wait_send()
    wait_for(both.at[1], part_send)
    wait_for(sums, sums_send)
    for ch in relays:
        pl.when(forwards(ch))(
            functools.partial(wait_for, via[ch], via_send.at[relays.index(ch)])
        )
    wait_for(early.at[others], early_send)
    wait_for(early.at[others], late_send)


def split(blocks, ys, ks):
    edge = max(1, blocks // 8)
    hops = RELAYS if ys == 2 and ks >= 6 and blocks >= 16 else ()
    inner = blocks - 2 * edge - sum(n for n, _ in hops)
    sizes = [max(1, edge // 2), *(n for n, _ in hops), inner - inner // 2, inner // 2 + edge - max(1, edge // 2), edge]
    ways = [None, *(way for _, way in hops), None, None, None]
    found = [(sum(sizes[:n]), size, ways[n]) for n, size in enumerate(sizes)]
    n = len(hops) + 1
    detours = [tuple(range(1, n))] if hops else []
    return found, [(0,), *detours, (n, n + 1, n + 2)], [(0,), (n,), (n + 1,), *[(m,) for m in range(1, n)], (n + 2,)]


def shards(ys, ks, grad_part, illum_part, source_count, rate, coef_table, coef_index):
    _, rows, lateral = grad_part.shape
    width = lateral // (2 * ys)
    blocks = width // LANES
    chunks, loads, turns = split(blocks, ys, ks)
    relays = [chunk for chunk in chunks if chunk[2]]
    f32, i32 = jnp.float32, jnp.int32
    dma = pltpu.SemaphoreType.DMA
    sent = pltpu.VMEM((ys - 1, 2, rows, width), f32)
    field = pltpu.VMEM((rows, width), f32)
    anywhere = pl.BlockSpec(memory_space=pl.ANY)
    small = (rate.reshape(1, -1), coef_table.reshape(1, -1), coef_index.reshape(1, -1))
    return pl.pallas_call(
        functools.partial(body, (ys, ks, rows, width, chunks, loads, turns)),
        out_shape=jax.ShapeDtypeStruct((rows, width), f32),
        in_specs=[anywhere] * 2 + [pl.BlockSpec(memory_space=pltpu.SMEM)] + [anywhere] * 3,
        out_specs=pl.BlockSpec(memory_space=pltpu.VMEM),
        scratch_shapes=[
            pltpu.VMEM((2, 2, rows, ys * width), f32),
            sent,
            sent,
            pltpu.VMEM((ks, 2, blocks, LANES), f32),
            field, field, field, field, field,
            pltpu.VMEM((2, blocks, LANES), f32),
            pltpu.VMEM(small[0].shape, f32),
            pltpu.VMEM(small[1].shape, f32),
            pltpu.VMEM(small[2].shape, i32),
            pltpu.SMEM((1,), i32),
            *[pltpu.VMEM((ks, 2 * sum(chunks[ch][1] for ch in group), LANES), f32) for group in turns],
            *[pltpu.VMEM((2, ys - 1, 2, rows, n * LANES), f32) for _, n, _ in relays],
            dma(((ys - 1) * len(loads) + 1,)),
            dma,
            dma,
            dma((len(chunks),)),
            dma((2, max(1, len(relays)))),
            dma((max(1, len(relays)),)),
            dma,
            dma,
            dma,
            dma((len(turns),)),
            dma,
            dma,
            dma((3,)),
            pltpu.SemaphoreType.REGULAR((ks // 2 + 2,)),
        ],
        compiler_params=pltpu.CompilerParams(collective_id=0, has_side_effects=True, vmem_limit_bytes=53 * 2**20),
    )(
        grad_part,
        illum_part,
        source_count,
        *[pltpu.with_memory_space_constraint(x, pltpu.HBM) for x in small],
    )


def solution(mesh):
    placed = (
        P("shot", "depth", None),
        P("shot", "depth", None),
        P("shot"),
        P("shot"),
        P(),
        P("depth"),
    )
    return jax.shard_map(
        functools.partial(shards, mesh.shape["shot"] // 2, mesh.shape["depth"]),
        mesh=mesh, in_specs=placed, out_specs=P("depth", "shot"), check_vma=False,
    )
```

```python
import functools

import jax
import jax.numpy as jnp
from jax import lax
from jax.experimental import pallas as pl
from jax.experimental.pallas import tpu as pltpu
from jax.sharding import PartitionSpec as P

MESH = pl.DeviceIdType.MESH
LANES = 128
SUB = 8


def deep(at, ks):
    return (at >= 2) & (at < ks)


def middle(at, ks):
    return (at >= 2) & (at < ks - 2)


def odd(at, ks):
    return lax.rem(at, 2) == 1


ROUTES = ((2, deep), (1, odd))
RELAYS = ((2, (2, deep)), (1, (2, middle)), (1, (1, odd)))


def body(
    dims,
    grad, illum, count, rate_hbm, table_hbm, index_hbm, out,
    both, sums, landed, early, inject, weigh, back, reach, held, states,
    rate, table, index, mate_count, *rest,
):
    ys, ks, rows, width, chunks, loads, turns = dims
    relays = [ch for ch in range(len(chunks)) if chunks[ch][2]]
    late, rest = rest[: len(turns)], rest[len(turns) :]
    via, rest = dict(zip(relays, rest)), rest[len(relays) :]
    (
        got, part_send, sums_send, sums_recv, via_recv, via_send,
        early_send, early_recv, late_send, late_recv, w_send, w_recv, small_sem, word,
    ) = rest
    tiles = rows // SUB
    me = lax.axis_index("shot")
    d = lax.axis_index("depth")
    y, c = me // 2, me % 2
    mate = y * 2 + 1 - c

    def peer(j):
        return j + (d <= j).astype(jnp.int32)

    def other(i):
        return lax.rem(y + i, ys)

    def greet(semaphore):
        flip = d + 1 - 2 * lax.rem(d, 2)
        pl.semaphore_signal(semaphore, inc=1, device_id=(me, flip), device_id_type=MESH)
        for step in (2, -2):
            near = d + step

            @pl.when((near >= 0) & (near < ks))
            def _():
                pl.semaphore_signal(semaphore, inc=1, device_id=(me, near), device_id_type=MESH)

    def neighbours():
        return (d >= 2).astype(jnp.int32) + (d < ks - 2).astype(jnp.int32) + 1

    def relayed(ch, at):
        return chunks[ch][2][1](at, ks)

    def stride(ch):
        return chunks[ch][2][0]

    barrier = pltpu.get_barrier_semaphore()
    pl.semaphore_signal(barrier, inc=1, device_id=(mate, d), device_id_type=MESH)
    for i in range(1, ys):
        pl.semaphore_signal(barrier, inc=1, device_id=(other(i) * 2 + c, d), device_id_type=MESH)
    pl.when(y == 0)(functools.partial(greet, barrier))
    expected = ys + (y == 0).astype(jnp.int32) * neighbours()
    for step, some in ROUTES if relays else ():
        expected = expected + some(d, ks).astype(jnp.int32) * (ys - 1)

        @pl.when((c == 1) & some(d + step, ks))
        def _():
            for i in range(1, ys):
                for own in range(2):
                    pl.semaphore_signal(
                        barrier, inc=1, device_id=(other(i) * 2 + own, d + step), device_id_type=MESH
                    )

    def reach_of(group):
        return chunks[group[0]][0], sum(chunks[ch][1] for ch in group)

    def columns(ch):
        return pl.ds(chunks[ch][0] * LANES, chunks[ch][1] * LANES)

    def fetch(i, start, cols, semaphore):
        into = pl.ds(i * width + start * LANES, cols * LANES)
        for a, src in enumerate((grad, illum)):
            at = pl.multiple_of((other(i) * 2 + c) * width + start * LANES, LANES)
            pltpu.make_async_copy(
                src.at[0, :, pl.ds(at, cols * LANES)], both.at[0, a, :, into], semaphore
            ).start()

    def give(i, start, cols, semaphore):
        into = pl.ds(i * width + start * LANES, cols * LANES)
        for a, src in enumerate((grad, illum)):
            at = pl.multiple_of((other(i) * 2 + 1 - c) * width + start * LANES, LANES)
            pltpu.make_async_remote_copy(
                src_ref=src.at[0, :, pl.ds(at, cols * LANES)],
                dst_ref=both.at[1, a, :, into],
                send_sem=part_send,
                recv_sem=semaphore,
                device_id=(mate, d),
                device_id_type=MESH,
            ).start()

    def wait_for(ref, semaphore):
        pltpu.make_async_copy(ref, ref, semaphore).wait()

    def arrived(i, start, cols, semaphore):
        wait_for(both.at[:, :, :, pl.ds(i * width + start * LANES, cols * LANES)], semaphore)

    def sums_copy(i, ch):
        return pltpu.make_async_remote_copy(
            src_ref=sums.at[i - 1, :, :, columns(ch)],
            dst_ref=landed.at[i - 1, :, :, columns(ch)],
            send_sem=sums_send,
            recv_sem=sums_recv.at[ch],
            device_id=(other(i) * 2 + c, d),
            device_id_type=MESH,
        )

    def relay_copy(i, ch):
        return pltpu.make_async_remote_copy(
            src_ref=sums.at[i - 1, :, :, columns(ch)],
            dst_ref=via[ch].at[c, i - 1],
            send_sem=sums_send,
            recv_sem=via_recv.at[c, relays.index(ch)],
            device_id=(other(i) * 2 + 1, d - stride(ch)),
            device_id_type=MESH,
        )

    def forwards(ch):
        return (c == 1) & relayed(ch, d + stride(ch))

    def forward(ch):
        @pl.when(forwards(ch))
        def _():
            for own in range(2):
                wait_for(via[ch].at[own], via_recv.at[own, relays.index(ch)])
                for i in range(1, ys):
                    pltpu.make_async_remote_copy(
                        src_ref=via[ch].at[own, i - 1],
                        dst_ref=landed.at[i - 1, :, :, columns(ch)],
                        send_sem=via_send.at[relays.index(ch)],
                        recv_sem=sums_recv.at[ch],
                        device_id=(y * 2 + own, d + stride(ch)),
                        device_id_type=MESH,
                    ).start()

    def carry_copy(buffer, send, recv, j):
        return pltpu.make_async_remote_copy(
            src_ref=buffer.at[d],
            dst_ref=buffer.at[d],
            send_sem=send,
            recv_sem=recv,
            device_id=(me, peer(j)),
            device_id_type=MESH,
        )

    w_copy = pltpu.make_async_remote_copy(
        src_ref=count,
        dst_ref=mate_count,
        send_sem=w_send,
        recv_sem=w_recv,
        device_id=(mate, d),
        device_id_type=MESH,
    )

    def small_copies():
        pairs = ((table_hbm, table), (index_hbm, index), (rate_hbm, rate))
        return [pltpu.make_async_copy(a, b, small_sem.at[n]) for n, (a, b) in enumerate(pairs)]

    first_part = [(i, group) for group in loads for i in range(1, ys)]
    fetch(1, *reach_of(loads[0]), got.at[0])

    pl.semaphore_wait(barrier, expected)
    w_copy.start()
    for n, (i, group) in enumerate(first_part):
        give(i, *reach_of(group), got.at[n])
    for n, (i, group) in enumerate(first_part[1:], 1):
        fetch(i, *reach_of(group), got.at[n])
    for copy in small_copies():
        copy.start()

    rounds = ks // 2
    pl.when(y == 0)(functools.partial(greet, word.at[0]))

    def pass_on(r):
        @pl.when(y == 0)
        def _():
            pl.semaphore_wait(word.at[r], neighbours())
            if r + 1 < rounds:
                greet(word.at[r + 1])
            else:
                for i in range(1, ys):
                    pl.semaphore_signal(
                        word.at[rounds], inc=1, device_id=(other(i) * 2 + c, d), device_id_type=MESH
                    )

        if r + 1 == rounds:
            pl.when(y != 0)(lambda: pl.semaphore_wait(word.at[rounds], 1))

    sub = lax.broadcasted_iota(jnp.int32, (SUB, LANES), 0)

    def prefix(v):
        for s in (1, 2, 4):
            v = v + jnp.where(sub >= s, pltpu.roll(v, s, 0), 0.0)
        return v

    def suffix(v):
        for s in (1, 2, 4):
            v = v + jnp.where(sub < SUB - s, pltpu.roll(v, SUB - s, 0), 0.0)
        return v

    def first(v):
        return jnp.broadcast_to(v[0:1], (SUB, LANES))

    def last(v):
        return jnp.broadcast_to(v[SUB - 1 : SUB], (SUB, LANES))

    entries = table.shape[1]

    def upright(row):
        n = row.shape[1]
        diagonal = lax.broadcasted_iota(jnp.int32, (n, n), 0) == lax.broadcasted_iota(
            jnp.int32, (n, n), 1
        )
        return jnp.sum(
            jnp.where(diagonal, jnp.broadcast_to(row, (n, n)), 0.0), axis=1, keepdims=True
        )

    def depths():
        level = lax.broadcasted_iota(jnp.int32, (entries, rows), 0)
        hit = jnp.broadcast_to(index[...], (entries, rows)) == level
        spread = jnp.broadcast_to(upright(table[...]), (entries, rows))
        picked = upright(jnp.sum(jnp.where(hit, spread, 0.0), axis=0, keepdims=True))
        coef, through, before = [], [], []
        total = jnp.zeros((SUB, LANES), jnp.float32)
        for t in range(tiles):
            v = jnp.broadcast_to(picked[t * SUB : (t + 1) * SUB], (SUB, LANES))
            run = prefix(v) + total
            coef.append(v)
            through.append(run)
            before.append(run - v)
            total = last(run)
        return coef, through, before, total

    def terms():
        coef, through, before, total = depths()
        for j in range(width // LANES):
            at = pl.ds(j * LANES, LANES)
            r = jnp.broadcast_to(rate[0:1, at], (SUB, LANES))
            tail = jnp.zeros((SUB, LANES), jnp.float32)
            for t in reversed(range(tiles)):
                zs = pl.ds(t * SUB, SUB)
                rest = 1.0 - jnp.exp(-(coef[t] * r))
                inject[zs, at] = rest * jnp.exp(through[t] * r)
                h = rest * jnp.exp(-((through[t] + before[t]) * r))
                weigh[zs, at] = h
                lift = jnp.exp(before[t] * r)
                back[zs, at] = lift
                run = suffix(h) + tail
                reach[zs, at] = lift * run
                tail = first(run)
            early[d, 0, pl.ds(j, 1), :] = jnp.exp(-(total * r))[0:1]
            early[d, 1, pl.ds(j, 1), :] = tail[0:1]

    def prepare():
        for copy in small_copies():
            copy.wait()
        terms()

    turn = word.at[rounds + 1]

    @pl.when(c == 1)
    def _():
        prepare()
        pl.semaphore_wait(turn, 1)

    w_copy.wait_recv()

    def weight(ref):
        return 1.0 / jnp.full((SUB, LANES), ref[0]).astype(jnp.float32)

    w, v = weight(count), weight(mate_count)

    def reduced(i, a, zs, at):
        at = pl.ds(i * width + at.start, at.size)
        if a == 0:
            return both[0, 0, zs, at] * w + both[1, 0, zs, at] * v
        return both[0, 1, zs, at] + both[1, 1, zs, at]

    def lanes(start, cols):
        return [pl.ds((start + j) * LANES, LANES) for j in range(cols)]

    for n, (i, group) in enumerate(first_part):
        arrived(i, *reach_of(group), got.at[n])
        for ch in group:
            for at in lanes(*chunks[ch][:2]):
                for t in range(tiles):
                    zs = pl.ds(t * SUB, SUB)
                    for a in range(2):
                        sums[i - 1, a, zs, at] = reduced(i, a, zs, at)
            if ch in relays:
                pl.when(relayed(ch, d))(relay_copy(i, ch).start)
                pl.when(jnp.logical_not(relayed(ch, d)))(sums_copy(i, ch).start)
            else:
                sums_copy(i, ch).start()

    local = len(first_part)
    fetch(0, 0, width // LANES, got.at[local])
    give(0, 0, width // LANES, got.at[local])

    @pl.when(c == 0)
    def _():
        prepare()
        pl.semaphore_signal(turn, inc=1, device_id=(mate, d), device_id_type=MESH)

    for r in range(rounds):
        pass_on(r)
    for r in relays:
        forward(r)
    for j in range(ks - 1):
        carry_copy(early, early_send, early_recv, j).start()

    arrived(0, 0, width // LANES, got.at[local])
    for n, group in enumerate(turns):
        start, cols = reach_of(group)
        for ch in group:
            wait_for(landed.at[:, :, :, columns(ch)], sums_recv.at[ch])
        for j, at in enumerate(lanes(start, cols)):
            carry = jnp.zeros((SUB, LANES), jnp.float32)
            parts = []
            for t in range(tiles):
                zs = pl.ds(t * SUB, SUB)
                num, den = reduced(0, 0, zs, at), reduced(0, 1, zs, at)
                for i in range(1, ys):
                    num = num + landed[i - 1, 0, zs, at]
                    den = den + landed[i - 1, 1, zs, at]
                run = prefix(inject[zs, at] * (num / den)) + carry
                parts.append(run)
                carry = last(run)
            row = pl.ds(start + j, 1)
            late[n][d, pl.ds(j, 1), :] = carry[0:1] * early[d, 0, row, :]
            tail = jnp.zeros((SUB, LANES), jnp.float32)
            for t in reversed(range(tiles)):
                zs = pl.ds(t * SUB, SUB)
                run = suffix(weigh[zs, at] * parts[t]) + tail
                held[zs, at] = run
                tail = first(run)
            late[n][d, pl.ds(cols + j, 1), :] = tail[0:1]
        for j in range(ks - 1):
            carry_copy(late[n], late_send, late_recv.at[int(n + 1 == len(turns))], j).start()

    others = pl.ds(0, ks - 1)
    wait_for(early.at[others], early_recv)
    for n, group in enumerate(turns):
        if n == 0:
            most = width // LANES - reach_of(turns[-1])[1]
            wait_for(early.at[others, :, pl.ds(0, most)], late_recv.at[0])
        if n + 1 == len(turns):
            wait_for(late[n].at[others], late_recv.at[1])
        start, cols = reach_of(group)
        rs = pl.ds(start, cols)
        down, lift = pl.ds(0, cols), pl.ds(cols, cols)
        state = jnp.zeros((cols, LANES), jnp.float32)
        mine = state
        ups = []
        for k in range(ks):
            mine = jnp.where(k == d, state, mine)
            ups.append(late[n][k, lift] + early[k, 1, rs] * state)
            if k < ks - 1:
                state = late[n][k, down] + early[k, 0, rs] * state
        up = jnp.zeros((cols, LANES), jnp.float32)
        for k in reversed(range(1, ks)):
            up = jnp.where(k > d, ups[k] + early[k, 0, rs] * up, up)
        states[0, rs] = mine
        states[1, rs] = up * early[d, 0, rs]
        for j, at in enumerate(lanes(start, cols)):
            row = pl.ds(start + j, 1)
            e = jnp.broadcast_to(states[0, row, :], (SUB, LANES))
            b = jnp.broadcast_to(states[1, row, :], (SUB, LANES))
            for t in range(tiles):
                zs = pl.ds(t * SUB, SUB)
                out[zs, at] = back[zs, at] * (held[zs, at] + b) + reach[zs, at] * e

    w_copy.wait_send()
    wait_for(both.at[1], part_send)
    wait_for(sums, sums_send)
    for ch in relays:
        pl.when(forwards(ch))(
            functools.partial(wait_for, via[ch], via_send.at[relays.index(ch)])
        )
    wait_for(early.at[others], early_send)
    wait_for(early.at[others], late_send)


def split(blocks, ys, ks):
    edge = max(1, blocks // 8)
    hops = RELAYS if ys == 2 and ks >= 6 and blocks >= 16 else ()
    inner = blocks - 2 * edge - sum(n for n, _ in hops)
    sizes = [max(1, edge // 2), *(n for n, _ in hops), inner - inner // 2, inner // 2 + edge - max(1, edge // 2), edge]
    ways = [None, *(way for _, way in hops), None, None, None]
    found = [(sum(sizes[:n]), size, ways[n]) for n, size in enumerate(sizes)]
    n = len(hops) + 1
    detours = [tuple(range(1, n))] if hops else []
    return found, [(0,), *detours, (n, n + 1, n + 2)], [(0,), (n,), (n + 1,), *[(m,) for m in range(1, n)], (n + 2,)]


def shards(ys, ks, grad_part, illum_part, source_count, rate, coef_table, coef_index):
    _, rows, lateral = grad_part.shape
    width = lateral // (2 * ys)
    blocks = width // LANES
    chunks, loads, turns = split(blocks, ys, ks)
    relays = [chunk for chunk in chunks if chunk[2]]
    f32, i32 = jnp.float32, jnp.int32
    dma = pltpu.SemaphoreType.DMA
    sent = pltpu.VMEM((ys - 1, 2, rows, width), f32)
    field = pltpu.VMEM((rows, width), f32)
    anywhere = pl.BlockSpec(memory_space=pl.ANY)
    small = (rate.reshape(1, -1), coef_table.reshape(1, -1), coef_index.reshape(1, -1))
    return pl.pallas_call(
        functools.partial(body, (ys, ks, rows, width, chunks, loads, turns)),
        out_shape=jax.ShapeDtypeStruct((rows, width), f32),
        in_specs=[anywhere] * 2 + [pl.BlockSpec(memory_space=pltpu.SMEM)] + [anywhere] * 3,
        out_specs=pl.BlockSpec(memory_space=pltpu.VMEM),
        scratch_shapes=[
            pltpu.VMEM((2, 2, rows, ys * width), f32),
            sent,
            sent,
            pltpu.VMEM((ks, 2, blocks, LANES), f32),
            field, field, field, field, field,
            pltpu.VMEM((2, blocks, LANES), f32),
            pltpu.VMEM(small[0].shape, f32),
            pltpu.VMEM(small[1].shape, f32),
            pltpu.VMEM(small[2].shape, i32),
            pltpu.SMEM((1,), i32),
            *[pltpu.VMEM((ks, 2 * sum(chunks[ch][1] for ch in group), LANES), f32) for group in turns],
            *[pltpu.VMEM((2, ys - 1, 2, rows, n * LANES), f32) for _, n, _ in relays],
            dma(((ys - 1) * len(loads) + 1,)),
            dma,
            dma,
            dma((len(chunks),)),
            dma((2, max(1, len(relays)))),
            dma((max(1, len(relays)),)),
            dma,
            dma,
            dma,
            dma((2,)),
            dma,
            dma,
            dma((3,)),
            pltpu.SemaphoreType.REGULAR((ks // 2 + 2,)),
        ],
        compiler_params=pltpu.CompilerParams(collective_id=0, has_side_effects=True, vmem_limit_bytes=53 * 2**20),
    )(
        grad_part,
        illum_part,
        source_count,
        *[pltpu.with_memory_space_constraint(x, pltpu.HBM) for x in small],
    )


def solution(mesh):
    placed = (
        P("shot", "depth", None),
        P("shot", "depth", None),
        P("shot"),
        P("shot"),
        P(),
        P("depth"),
    )
    return jax.shard_map(
        functools.partial(shards, mesh.shape["shot"] // 2, mesh.shape["depth"]),
        mesh=mesh, in_specs=placed, out_specs=P("depth", "shot"), check_vma=False,
    )
```

```python
import functools

import jax
import jax.numpy as jnp
from jax import lax
from jax.experimental import pallas as pl
from jax.experimental.pallas import tpu as pltpu
from jax.sharding import PartitionSpec as P

MESH = pl.DeviceIdType.MESH
LANES = 128
SUB = 8


def deep(at, ks):
    return (at >= 2) & (at < ks)


def middle(at, ks):
    return (at >= 2) & (at < ks - 2)


def odd(at, ks):
    return lax.rem(at, 2) == 1


ROUTES = ((2, deep), (1, odd))
RELAYS = ((2, (2, deep)), (1, (2, middle)), (1, (1, odd)))


def body(
    dims,
    grad, illum, count, rate_hbm, table_hbm, index_hbm, out,
    both, sums, landed, early, inject, weigh, back, reach, held, states,
    rate, table, index, mate_count, *rest,
):
    ys, ks, rows, width, chunks, loads, turns = dims
    relays = [ch for ch in range(len(chunks)) if chunks[ch][2]]
    late, rest = rest[: len(turns)], rest[len(turns) :]
    via, rest = dict(zip(relays, rest)), rest[len(relays) :]
    (
        got, part_send, sums_send, sums_recv, via_recv, via_send,
        early_send, early_recv, late_send, late_recv, w_send, w_recv, small_sem, word,
    ) = rest
    tiles = rows // SUB
    me = lax.axis_index("shot")
    d = lax.axis_index("depth")
    y, c = me // 2, me % 2
    mate = y * 2 + 1 - c

    def peer(j):
        return j + (d <= j).astype(jnp.int32)

    def other(i):
        return lax.rem(y + i, ys)

    def greet(semaphore):
        flip = d + 1 - 2 * lax.rem(d, 2)
        pl.semaphore_signal(semaphore, inc=1, device_id=(me, flip), device_id_type=MESH)
        for step in (2, -2):
            near = d + step

            @pl.when((near >= 0) & (near < ks))
            def _():
                pl.semaphore_signal(semaphore, inc=1, device_id=(me, near), device_id_type=MESH)

    def neighbours():
        return (d >= 2).astype(jnp.int32) + (d < ks - 2).astype(jnp.int32) + 1

    def relayed(ch, at):
        return chunks[ch][2][1](at, ks)

    def stride(ch):
        return chunks[ch][2][0]

    barrier = pltpu.get_barrier_semaphore()
    pl.semaphore_signal(barrier, inc=1, device_id=(mate, d), device_id_type=MESH)
    for i in range(1, ys):
        pl.semaphore_signal(barrier, inc=1, device_id=(other(i) * 2 + c, d), device_id_type=MESH)
    pl.when(y == 0)(functools.partial(greet, barrier))
    expected = ys + (y == 0).astype(jnp.int32) * neighbours()
    for step, some in ROUTES if relays else ():
        expected = expected + some(d, ks).astype(jnp.int32) * (ys - 1)

        @pl.when(some(d + step, ks))
        def _():
            for i in range(1, ys):
                pl.semaphore_signal(barrier, inc=1, device_id=(other(i) * 2 + c, d + step), device_id_type=MESH)

    def reach_of(group):
        return chunks[group[0]][0], sum(chunks[ch][1] for ch in group)

    def columns(ch):
        return pl.ds(chunks[ch][0] * LANES, chunks[ch][1] * LANES)

    def fetch(i, start, cols, semaphore):
        into = pl.ds(i * width + start * LANES, cols * LANES)
        for a, src in enumerate((grad, illum)):
            at = pl.multiple_of((other(i) * 2 + c) * width + start * LANES, LANES)
            pltpu.make_async_copy(
                src.at[0, :, pl.ds(at, cols * LANES)], both.at[0, a, :, into], semaphore
            ).start()

    def give(i, start, cols, semaphore):
        into = pl.ds(i * width + start * LANES, cols * LANES)
        for a, src in enumerate((grad, illum)):
            at = pl.multiple_of((other(i) * 2 + 1 - c) * width + start * LANES, LANES)
            pltpu.make_async_remote_copy(
                src_ref=src.at[0, :, pl.ds(at, cols * LANES)],
                dst_ref=both.at[1, a, :, into],
                send_sem=part_send,
                recv_sem=semaphore,
                device_id=(mate, d),
                device_id_type=MESH,
            ).start()

    def wait_for(ref, semaphore):
        pltpu.make_async_copy(ref, ref, semaphore).wait()

    def arrived(i, start, cols, semaphore):
        wait_for(both.at[:, :, :, pl.ds(i * width + start * LANES, cols * LANES)], semaphore)

    def sums_copy(i, ch):
        return pltpu.make_async_remote_copy(
            src_ref=sums.at[i - 1, :, :, columns(ch)],
            dst_ref=landed.at[i - 1, :, :, columns(ch)],
            send_sem=sums_send,
            recv_sem=sums_recv.at[ch],
            device_id=(other(i) * 2 + c, d),
            device_id_type=MESH,
        )

    def relay_copy(i, ch):
        return pltpu.make_async_remote_copy(
            src_ref=sums.at[i - 1, :, :, columns(ch)],
            dst_ref=via[ch].at[i - 1],
            send_sem=sums_send,
            recv_sem=via_recv.at[relays.index(ch)],
            device_id=(other(i) * 2 + c, d - stride(ch)),
            device_id_type=MESH,
        )

    def forward(ch):
        @pl.when(relayed(ch, d + stride(ch)))
        def _():
            wait_for(via[ch], via_recv.at[relays.index(ch)])
            for i in range(1, ys):
                pltpu.make_async_remote_copy(
                    src_ref=via[ch].at[i - 1],
                    dst_ref=landed.at[i - 1, :, :, columns(ch)],
                    send_sem=via_send.at[relays.index(ch)],
                    recv_sem=sums_recv.at[ch],
                    device_id=(me, d + stride(ch)),
                    device_id_type=MESH,
                ).start()

    def carry_copy(buffer, send, recv, j):
        return pltpu.make_async_remote_copy(
            src_ref=buffer.at[d],
            dst_ref=buffer.at[d],
            send_sem=send,
            recv_sem=recv,
            device_id=(me, peer(j)),
            device_id_type=MESH,
        )

    w_copy = pltpu.make_async_remote_copy(
        src_ref=count,
        dst_ref=mate_count,
        send_sem=w_send,
        recv_sem=w_recv,
        device_id=(mate, d),
        device_id_type=MESH,
    )

    def small_copies():
        pairs = ((table_hbm, table), (index_hbm, index), (rate_hbm, rate))
        return [pltpu.make_async_copy(a, b, small_sem.at[n]) for n, (a, b) in enumerate(pairs)]

    first_part = [(i, group) for group in loads for i in range(1, ys)]
    fetch(1, *reach_of(loads[0]), got.at[0])

    pl.semaphore_wait(barrier, expected)
    w_copy.start()
    for n, (i, group) in enumerate(first_part):
        give(i, *reach_of(group), got.at[n])
    for n, (i, group) in enumerate(first_part[1:], 1):
        fetch(i, *reach_of(group), got.at[n])
    for copy in small_copies():
        copy.start()

    rounds = ks // 2
    pl.when(y == 0)(functools.partial(greet, word.at[0]))

    def pass_on(r):
        @pl.when(y == 0)
        def _():
            pl.semaphore_wait(word.at[r], neighbours())
            if r + 1 < rounds:
                greet(word.at[r + 1])
            else:
                for i in range(1, ys):
                    pl.semaphore_signal(
                        word.at[rounds], inc=1, device_id=(other(i) * 2 + c, d), device_id_type=MESH
                    )

        if r + 1 == rounds:
            pl.when(y != 0)(lambda: pl.semaphore_wait(word.at[rounds], 1))

    sub = lax.broadcasted_iota(jnp.int32, (SUB, LANES), 0)

    def prefix(v):
        for s in (1, 2, 4):
            v = v + jnp.where(sub >= s, pltpu.roll(v, s, 0), 0.0)
        return v

    def suffix(v):
        for s in (1, 2, 4):
            v = v + jnp.where(sub < SUB - s, pltpu.roll(v, SUB - s, 0), 0.0)
        return v

    def first(v):
        return jnp.broadcast_to(v[0:1], (SUB, LANES))

    def last(v):
        return jnp.broadcast_to(v[SUB - 1 : SUB], (SUB, LANES))

    entries = table.shape[1]

    def upright(row):
        n = row.shape[1]
        diagonal = lax.broadcasted_iota(jnp.int32, (n, n), 0) == lax.broadcasted_iota(
            jnp.int32, (n, n), 1
        )
        return jnp.sum(
            jnp.where(diagonal, jnp.broadcast_to(row, (n, n)), 0.0), axis=1, keepdims=True
        )

    def depths():
        level = lax.broadcasted_iota(jnp.int32, (entries, rows), 0)
        hit = jnp.broadcast_to(index[...], (entries, rows)) == level
        spread = jnp.broadcast_to(upright(table[...]), (entries, rows))
        picked = upright(jnp.sum(jnp.where(hit, spread, 0.0), axis=0, keepdims=True))
        coef, through, before = [], [], []
        total = jnp.zeros((SUB, LANES), jnp.float32)
        for t in range(tiles):
            v = jnp.broadcast_to(picked[t * SUB : (t + 1) * SUB], (SUB, LANES))
            run = prefix(v) + total
            coef.append(v)
            through.append(run)
            before.append(run - v)
            total = last(run)
        return coef, through, before, total

    def terms():
        coef, through, before, total = depths()
        for j in range(width // LANES):
            at = pl.ds(j * LANES, LANES)
            r = jnp.broadcast_to(rate[0:1, at], (SUB, LANES))
            tail = jnp.zeros((SUB, LANES), jnp.float32)
            for t in reversed(range(tiles)):
                zs = pl.ds(t * SUB, SUB)
                rest = 1.0 - jnp.exp(-(coef[t] * r))
                inject[zs, at] = rest * jnp.exp(through[t] * r)
                h = rest * jnp.exp(-((through[t] + before[t]) * r))
                weigh[zs, at] = h
                lift = jnp.exp(before[t] * r)
                back[zs, at] = lift
                run = suffix(h) + tail
                reach[zs, at] = lift * run
                tail = first(run)
            early[d, 0, pl.ds(j, 1), :] = jnp.exp(-(total * r))[0:1]
            early[d, 1, pl.ds(j, 1), :] = tail[0:1]

    def prepare():
        for copy in small_copies():
            copy.wait()
        terms()

    turn = word.at[rounds + 1]

    @pl.when(c == 1)
    def _():
        prepare()
        pl.semaphore_wait(turn, 1)

    w_copy.wait_recv()

    def weight(ref):
        return 1.0 / jnp.full((SUB, LANES), ref[0]).astype(jnp.float32)

    w, v = weight(count), weight(mate_count)

    def reduced(i, a, zs, at):
        at = pl.ds(i * width + at.start, at.size)
        if a == 0:
            return both[0, 0, zs, at] * w + both[1, 0, zs, at] * v
        return both[0, 1, zs, at] + both[1, 1, zs, at]

    def lanes(start, cols):
        return [pl.ds((start + j) * LANES, LANES) for j in range(cols)]

    for n, (i, group) in enumerate(first_part):
        arrived(i, *reach_of(group), got.at[n])
        for ch in group:
            for at in lanes(*chunks[ch][:2]):
                for t in range(tiles):
                    zs = pl.ds(t * SUB, SUB)
                    for a in range(2):
                        sums[i - 1, a, zs, at] = reduced(i, a, zs, at)
            if ch in relays:
                pl.when(relayed(ch, d))(relay_copy(i, ch).start)
                pl.when(jnp.logical_not(relayed(ch, d)))(sums_copy(i, ch).start)
            else:
                sums_copy(i, ch).start()

    local = len(first_part)
    fetch(0, 0, width // LANES, got.at[local])
    give(0, 0, width // LANES, got.at[local])

    @pl.when(c == 0)
    def _():
        prepare()
        pl.semaphore_signal(turn, inc=1, device_id=(mate, d), device_id_type=MESH)

    for r in range(rounds):
        pass_on(r)
    for r in relays:
        forward(r)
    for j in range(ks - 1):
        carry_copy(early, early_send, early_recv, j).start()

    arrived(0, 0, width // LANES, got.at[local])
    for n, group in enumerate(turns):
        start, cols = reach_of(group)
        for ch in group:
            wait_for(landed.at[:, :, :, columns(ch)], sums_recv.at[ch])
        for j, at in enumerate(lanes(start, cols)):
            carry = jnp.zeros((SUB, LANES), jnp.float32)
            parts = []
            for t in range(tiles):
                zs = pl.ds(t * SUB, SUB)
                num, den = reduced(0, 0, zs, at), reduced(0, 1, zs, at)
                for i in range(1, ys):
                    num = num + landed[i - 1, 0, zs, at]
                    den = den + landed[i - 1, 1, zs, at]
                run = prefix(inject[zs, at] * (num / den)) + carry
                parts.append(run)
                carry = last(run)
            row = pl.ds(start + j, 1)
            late[n][d, pl.ds(j, 1), :] = carry[0:1] * early[d, 0, row, :]
            tail = jnp.zeros((SUB, LANES), jnp.float32)
            for t in reversed(range(tiles)):
                zs = pl.ds(t * SUB, SUB)
                run = suffix(weigh[zs, at] * parts[t]) + tail
                held[zs, at] = run
                tail = first(run)
            late[n][d, pl.ds(cols + j, 1), :] = tail[0:1]
        for j in range(ks - 1):
            carry_copy(late[n], late_send, late_recv.at[int(n + 1 == len(turns))], j).start()

    others = pl.ds(0, ks - 1)
    wait_for(early.at[others], early_recv)
    for n, group in enumerate(turns):
        if n == 0:
            most = width // LANES - reach_of(turns[-1])[1]
            wait_for(early.at[others, :, pl.ds(0, most)], late_recv.at[0])
        if n + 1 == len(turns):
            wait_for(late[n].at[others], late_recv.at[1])
        start, cols = reach_of(group)
        rs = pl.ds(start, cols)
        down, lift = pl.ds(0, cols), pl.ds(cols, cols)
        state = jnp.zeros((cols, LANES), jnp.float32)
        mine = state
        ups = []
        for k in range(ks):
            mine = jnp.where(k == d, state, mine)
            ups.append(late[n][k, lift] + early[k, 1, rs] * state)
            if k < ks - 1:
                state = late[n][k, down] + early[k, 0, rs] * state
        up = jnp.zeros((cols, LANES), jnp.float32)
        for k in reversed(range(1, ks)):
            up = jnp.where(k > d, ups[k] + early[k, 0, rs] * up, up)
        states[0, rs] = mine
        states[1, rs] = up * early[d, 0, rs]
        for j, at in enumerate(lanes(start, cols)):
            row = pl.ds(start + j, 1)
            e = jnp.broadcast_to(states[0, row, :], (SUB, LANES))
            b = jnp.broadcast_to(states[1, row, :], (SUB, LANES))
            for t in range(tiles):
                zs = pl.ds(t * SUB, SUB)
                out[zs, at] = back[zs, at] * (held[zs, at] + b) + reach[zs, at] * e

    w_copy.wait_send()
    wait_for(both.at[1], part_send)
    wait_for(sums, sums_send)
    for ch in relays:
        pl.when(relayed(ch, d + stride(ch)))(
            functools.partial(wait_for, via[ch], via_send.at[relays.index(ch)])
        )
    wait_for(early.at[others], early_send)
    wait_for(early.at[others], late_send)


def split(blocks, ys, ks):
    edge = max(1, blocks // 8)
    hops = RELAYS if ys == 2 and ks >= 6 and blocks >= 16 else ()
    inner = blocks - 2 * edge - sum(n for n, _ in hops)
    sizes = [max(1, edge // 2), *(n for n, _ in hops), inner - inner // 2, inner // 2 + edge - max(1, edge // 2), edge]
    ways = [None, *(way for _, way in hops), None, None, None]
    found = [(sum(sizes[:n]), size, ways[n]) for n, size in enumerate(sizes)]
    n = len(hops) + 1
    detours = [tuple(range(1, n))] if hops else []
    return found, [(0,), *detours, (n, n + 1, n + 2)], [(0,), (n,), (n + 1,), *[(m,) for m in range(1, n)], (n + 2,)]


def shards(ys, ks, grad_part, illum_part, source_count, rate, coef_table, coef_index):
    _, rows, lateral = grad_part.shape
    width = lateral // (2 * ys)
    blocks = width // LANES
    chunks, loads, turns = split(blocks, ys, ks)
    relays = [chunk for chunk in chunks if chunk[2]]
    f32, i32 = jnp.float32, jnp.int32
    dma = pltpu.SemaphoreType.DMA
    sent = pltpu.VMEM((ys - 1, 2, rows, width), f32)
    field = pltpu.VMEM((rows, width), f32)
    anywhere = pl.BlockSpec(memory_space=pl.ANY)
    small = (rate.reshape(1, -1), coef_table.reshape(1, -1), coef_index.reshape(1, -1))
    return pl.pallas_call(
        functools.partial(body, (ys, ks, rows, width, chunks, loads, turns)),
        out_shape=jax.ShapeDtypeStruct((rows, width), f32),
        in_specs=[anywhere] * 2 + [pl.BlockSpec(memory_space=pltpu.SMEM)] + [anywhere] * 3,
        out_specs=pl.BlockSpec(memory_space=pltpu.VMEM),
        scratch_shapes=[
            pltpu.VMEM((2, 2, rows, ys * width), f32),
            sent,
            sent,
            pltpu.VMEM((ks, 2, blocks, LANES), f32),
            field, field, field, field, field,
            pltpu.VMEM((2, blocks, LANES), f32),
            pltpu.VMEM(small[0].shape, f32),
            pltpu.VMEM(small[1].shape, f32),
            pltpu.VMEM(small[2].shape, i32),
            pltpu.SMEM((1,), i32),
            *[pltpu.VMEM((ks, 2 * sum(chunks[ch][1] for ch in group), LANES), f32) for group in turns],
            *[pltpu.VMEM((ys - 1, 2, rows, n * LANES), f32) for _, n, _ in relays],
            dma(((ys - 1) * len(loads) + 1,)),
            dma,
            dma,
            dma((len(chunks),)),
            dma((max(1, len(relays)),)),
            dma((max(1, len(relays)),)),
            dma,
            dma,
            dma,
            dma((2,)),
            dma,
            dma,
            dma((3,)),
            pltpu.SemaphoreType.REGULAR((ks // 2 + 2,)),
        ],
        compiler_params=pltpu.CompilerParams(collective_id=0, has_side_effects=True, vmem_limit_bytes=53 * 2**20),
    )(
        grad_part,
        illum_part,
        source_count,
        *[pltpu.with_memory_space_constraint(x, pltpu.HBM) for x in small],
    )


def solution(mesh):
    placed = (
        P("shot", "depth", None),
        P("shot", "depth", None),
        P("shot"),
        P("shot"),
        P(),
        P("depth"),
    )
    return jax.shard_map(
        functools.partial(shards, mesh.shape["shot"] // 2, mesh.shape["depth"]),
        mesh=mesh, in_specs=placed, out_specs=P("depth", "shot"), check_vma=False,
    )
```
